256 devices in a mesh: frames: 8 (over y, x_lo), labels: 8 (over z), hidden: 4 (over x_hi, core).
Axes of the slice: x: 4 (x_hi: 2, x_lo: 2; x = x_hi * 2 + x_lo), y: 4, z: 8, core: 2. Of those that a mesh axis runs over, the one named last changes fastest.
Arguments:
- features: bfloat16 [1024, 1024], P('frames'), may hold values from -6 to 6
- up_weight: bfloat16 [1024, 4096], P(None, 'hidden'), may hold values from -0.1875 to 0.1875
- down_weight: bfloat16 [4096, 640], P('hidden'), may hold values from -0.09375 to 0.09375
- predictor: bfloat16 [512, 640], P(('labels', 'hidden')), may hold values from -4 to 4
- out_weight: bfloat16 [640, 1024], replicated, may hold values from -1.1 to 1.1
- blank_weight: float32 [1024, 512], P('frames', ('labels', 'hidden')), may hold values from 0 to 0.06
- label_weight: float32 [1024, 512], P('frames', ('labels', 'hidden')), may hold values from 0 to 0.06
- targets: int32 [512], P(('labels', 'hidden')), may hold values from 1 to 1023
Outputs:
- enc_grad: float32 [1024, 640], P(('frames', 'labels', 'hidden'))
- pred_grad: float32 [512, 640], P(('labels', 'hidden'))
- head_grad: float32 [1024, 640], P(('frames', 'labels', 'hidden'))
The draws below stay inside these ranges and needn't reach their ends.
All inputs are finite; a program needn't handle non-finite values.
Results may differ from the reference program's by a relative error of at most 0.0023.
Values sent between devices are 32-bit elements; how exact they have to be, the bound alone decides.
A program may use at most 64 MiB of HBM per device.

```python
import math
import jax
import jax.numpy as jnp
from jax import lax

DIN = 1024
HID = 4096
JD = 640
VOCAB = 1024
SEQ_T = 1024
SEQ_U = 512


def draw_out_weight(key, part):
    matrix = jnp.clip(jax.random.normal(jax.random.fold_in(key, 11), (JD, VOCAB), jnp.float32), -6.0, 6.0) * 0.17
    return matrix.astype(jnp.bfloat16)


def draw_predictor(key, part):
    matrix = jnp.clip(jax.random.normal(jax.random.fold_in(key, 12), (SEQ_U, JD), jnp.float32), -4.0, 4.0)
    return matrix.astype(jnp.bfloat16)


def touch_ends(drawn, key, smallest, largest):
    index_at = [jax.random.randint(jax.random.fold_in(key, axis), (), 0, length) for axis, length in enumerate(drawn.shape)]
    main_axis = drawn.shape.index(max(drawn.shape))
    neighbour = index_at[:main_axis] + [(index_at[main_axis] + 1) % drawn.shape[main_axis]] + index_at[main_axis + 1:]
    return drawn.at[tuple(index_at)].set(smallest).at[tuple(neighbour)].set(largest)


def levels(key, shape, split, smallest, high):
    def one(axis_at, blocks):
        steps = jax.random.uniform(jax.random.fold_in(jax.random.fold_in(key, 6), axis_at), (blocks,), jnp.float32, smallest / len(split), high / len(split))
        return jnp.repeat(jnp.exp(steps), shape[axis_at] // blocks).reshape((-1,) + (1,) * (len(shape) - axis_at - 1))

    factor_of = one(*split[0])
    for cut in split[1:]:
        factor_of = factor_of * one(*cut)
    return factor_of


def normal_values(rng, extent, width, bound, shards=(), kind=jnp.bfloat16):
    values = width * jax.random.normal(rng, extent, jnp.float32)
    if shards:
        values = values * levels(rng, extent, shards, -0.22, 0.18)
    return jnp.clip(values, -bound, bound).astype(kind)


def setup_inputs(seed: int = 0) -> dict:
    arg_keys = jax.random.split(jax.random.key(seed), 9)
    return {
        "features": normal_values(arg_keys[0], (SEQ_T, DIN), 1.0, 6.0, ((0, 8),)),
        "up_weight": normal_values(arg_keys[1], (DIN, HID), DIN ** -0.5, 0.1875, ((1, 4),)),
        "down_weight": normal_values(arg_keys[2], (HID, JD), HID ** -0.5, 0.09375, ((0, 4),)),
        "predictor": draw_predictor(jax.random.fold_in(arg_keys[8], 71), 0),
        "out_weight": draw_out_weight(jax.random.fold_in(arg_keys[8], 71), 0),
        "blank_weight": jnp.clip(0.06 * jax.random.uniform(arg_keys[5], (SEQ_T, SEQ_U), jnp.float32) ** levels(arg_keys[5], (SEQ_T, SEQ_U), ((0, 8), (1, 32)), -0.2, 0.2), 0.0, 0.06),
        "label_weight": jnp.clip(0.06 * jax.random.uniform(arg_keys[6], (SEQ_T, SEQ_U), jnp.float32) ** levels(arg_keys[6], (SEQ_T, SEQ_U), ((0, 8), (1, 32)), -0.2, 0.2), 0.0, 0.06),
        "targets": touch_ends(jax.random.randint(arg_keys[7], (SEQ_U,), 1, VOCAB), jax.random.fold_in(arg_keys[7], 1), 1, VOCAB - 1).astype(jnp.int32),
    }


def reference(features, up_weight, down_weight, predictor, out_weight, blank_weight, label_weight, targets):
    hidden_act = jax.nn.relu(jnp.dot(features, up_weight, preferred_element_type=jnp.float32)).astype(jnp.bfloat16)
    encoded = jnp.dot(hidden_act, down_weight, preferred_element_type=jnp.float32)
    pred_wide = predictor.astype(jnp.float32)
    vocab_ids = jnp.arange(VOCAB, dtype=jnp.int32)
    label_hot = (targets[:, None] == vocab_ids[None, :]).astype(jnp.float32)
    blank_hot = (vocab_ids == 0).astype(jnp.float32)
    block_rows = 8

    def joint_step(carry, inputs):
        head_sum, pred_sum = carry
        enc_block, blank_block, label_block = inputs
        joint_cells = jnp.tanh(enc_block[:, None, :] + pred_wide[None, :, :]).astype(jnp.bfloat16)
        joint_cells = joint_cells.reshape(block_rows * SEQ_U, JD)
        logits = jnp.dot(joint_cells, out_weight, preferred_element_type=jnp.float32)
        top_logit = lax.optimization_barrier(jnp.max(logits, axis=1, keepdims=True))
        log_total = top_logit + jnp.log(lax.optimization_barrier(jnp.sum(jnp.exp(logits - top_logit), axis=1, keepdims=True)))
        probs = jnp.exp(logits - log_total)
        blank_flat = blank_block.reshape(-1, 1)
        label_flat = label_block.reshape(-1, 1)
        cell_hot = jnp.broadcast_to(label_hot[None], (block_rows, SEQ_U, VOCAB)).reshape(-1, VOCAB)
        logit_grad = ((blank_flat + label_flat) * probs - blank_flat * blank_hot - label_flat * cell_hot).astype(jnp.bfloat16)
        joint_grad = lax.dot_general(logit_grad, out_weight, (((1,), (1,)), ((), ())), preferred_element_type=jnp.float32)
        cells_wide = joint_cells.astype(jnp.float32)
        tanh_grad = (joint_grad * (1.0 - cells_wide * cells_wide)).reshape(block_rows, SEQ_U, JD)
        head_sum = head_sum + lax.dot_general(logit_grad, joint_cells, (((0,), (0,)), ((), ())), preferred_element_type=jnp.float32)
        return ((head_sum, pred_sum + lax.optimization_barrier(jnp.sum(tanh_grad, axis=0))), lax.optimization_barrier(jnp.sum(tanh_grad, axis=1)))
    inputs = (encoded.reshape(-1, block_rows, JD), blank_weight.reshape(-1, block_rows, SEQ_U), label_weight.reshape(-1, block_rows, SEQ_U))
    start = (jnp.zeros((VOCAB, JD), jnp.float32), jnp.zeros((SEQ_U, JD), jnp.float32))
    (head_sum, pred_sum), enc_parts = lax.scan(joint_step, start, inputs)
    return (enc_parts.reshape(SEQ_T, JD), pred_sum, head_sum / math.sqrt(SEQ_T * SEQ_U))
```

```python
import math

import jax
import jax.numpy as jnp
from jax import lax
from jax.experimental import pallas as pl
from jax.experimental.pallas import tpu as pltpu
from jax.sharding import PartitionSpec as P

F32 = jnp.float32
BF16 = jnp.bfloat16
JD = 640
VOCAB = 1024
CH = 4
FT = 8
LB = 64
CELLS = FT * LB
RB = 16
SCALE = 1.0 / math.sqrt(1024 * 512)


def send(src, dst, send_sem, recv_sem, device):
    pltpu.make_async_remote_copy(
        src_ref=src,
        dst_ref=dst,
        send_sem=send_sem,
        recv_sem=recv_sem,
        device_id=device,
        device_id_type=pl.DeviceIdType.MESH,
    ).start()


def drain(ref, sem):
    pltpu.make_async_copy(ref, ref, sem).wait()


def kernel(
    feat_hbm, up_hbm, down_hbm, pred_in, w_hbm, blank_in, label_in, targets,
    enc_out, pred_out, head_out,
    feat, up, down, w, load_sem,
    msg, msg_r, msg_ss, msg_rs,
    part, part_r, part_ss, part_rs,
    pred64, wsum, wblank, wlabel, tgt64,
    joint, lg, grad, jg,
    encp, encp_r, encp_ss, encp_rs,
    predp, predp_r, predp_ss, predp_rs,
    predb, predb_r, predb_ss, predb_rs,
    hab, hc, h1ab, h1c, h1ab_ss, h1ab_rs, h1c_ss, h1c_rs,
    p1a, p1b, p1c, p1_ss, p1_rs,
    a1, b1, c1, p2a, p2b, p2c, p2_ss, p2_rs,
    ab2, c2, p3ab, p3c, p3_ss, p3_rs,
    fin, fin_ss, fin_rs,
):
    f = lax.axis_index("frames")
    z = lax.axis_index("labels")
    h = lax.axis_index("hidden")
    y, x_lo = f // 2, f % 2
    x_hi, core = h // 2, h % 2
    x = x_hi * 2 + x_lo

    loads = []
    for n, (a, b) in enumerate(((feat_hbm, feat), (up_hbm, up), (down_hbm, down), (w_hbm, w))):
        cp = pltpu.make_async_copy(a, b, load_sem.at[n])
        cp.start()
        loads.append(cp)

    def h_peer(k):
        return {"hidden": (h + k) % 4}

    def z_peer(k):
        return {"labels": (z + k) % 8}

    def y_peer(k):
        return {"frames": ((y + k) % 4) * 2 + x_lo}

    def x_peer(k):
        xx = (x + k) % 4
        return {"frames": y * 2 + xx % 2, "hidden": (xx // 2) * 2 + core}

    def f_peer(k):
        return {"frames": (f + k) % 8}

    partner = {"hidden": x_hi * 2 + (1 - core)}

    barrier = pltpu.get_barrier_semaphore()
    greeted = [h_peer(k) for k in (1, 2, 3)] + [z_peer(k) for k in range(1, 8)]
    greeted += [f_peer(k) for k in range(1, 8)] + [x_peer(k) for k in (1, 3)]
    for device in greeted:
        pl.semaphore_signal(barrier, inc=1, device_id=device, device_id_type=pl.DeviceIdType.MESH)

    wcat = jnp.concatenate([blank_in[...], label_in[...]], axis=0)
    row = lax.broadcasted_iota(jnp.int32, (256, 128), 0)
    lane = lax.broadcasted_iota(jnp.int32, (256, 128), 1)
    slot = lane % 32
    tcol = jnp.zeros((16, 128), jnp.int32)
    trow = lax.broadcasted_iota(jnp.int32, (16, 128), 0)
    tlane = lax.broadcasted_iota(jnp.int32, (16, 128), 1)
    for i in range(16):
        tcol = jnp.where(trow == i, targets[i], tcol)
    tfloat = jnp.where(tlane == 64, tcol.astype(F32), 0.0)
    pred_wide = pred_in[...].astype(F32)
    for k in range(4):
        peer = (h + k) % 4
        frame = (slot // 4) * 16 + peer * 4 + slot % 4
        pick = ((row // 128) == (lane // 32)) & ((row % 128) == frame)
        moved = lax.dot_general(
            wcat, pick.astype(F32), (((0,), (0,)), ((), ())),
            preferred_element_type=F32, precision=lax.Precision.HIGHEST,
        )
        msg[k, :, 0:JD] = pred_wide
        msg[k, :, JD:JD + 128] = moved + tfloat

    prow = lax.broadcasted_iota(jnp.int32, (128, 128), 0)
    pcol = lax.broadcasted_iota(jnp.int32, (128, 128), 1)
    pr = prow % 8
    pframe = ((prow // 32) * 2 + pr // 4) * 16 + ((h + (prow // 8) % 4) % 4) * 4 + pr % 4
    perm = (pcol == pframe).astype(F32).astype(BF16)
    loads[0].wait()
    feat_p = jnp.dot(perm, feat[...], preferred_element_type=F32).astype(BF16)

    pl.semaphore_wait(barrier, len(greeted))
    for k in (1, 2, 3):
        send(msg.at[k], msg_r.at[k - 1], msg_ss, msg_rs, h_peer(k))

    loads[1].wait()
    hidden = jnp.maximum(jnp.dot(feat_p, up[...], preferred_element_type=F32), 0.0).astype(BF16)
    loads[2].wait()
    enc = jnp.dot(hidden, down[...], preferred_element_type=F32)
    for c in range(CH):
        for k in range(4):
            r = c * 32 + k * 8
            part[c, k] = enc[r:r + 8, :]
    for c in range(CH):
        for k in (1, 2, 3):
            send(part.at[c, k], part_r.at[c, k - 1], part_ss, part_rs.at[c], h_peer(k))

    drain(msg_r, msg_rs)
    for k in range(4):
        src = msg.at[0] if k == 0 else msg_r.at[k - 1]
        rows = slice(k * 16, k * 16 + 16)
        pred64[rows, :] = src[:, 0:JD]
        tail = src[:, JD:JD + 128]
        tgt64[rows, :] = jnp.broadcast_to(tail[:, 64:65], (16, 128))
        for t in range(CH * FT):
            r = t * LB + k * 16
            b = jnp.broadcast_to(tail[:, t:t + 1], (16, 128))
            l = jnp.broadcast_to(tail[:, 32 + t:33 + t], (16, 128))
            wsum[r:r + 16, :] = b + l
            wblank[r:r + 16, :] = b
            wlabel[r:r + 16, :] = l
    loads[3].wait()

    vocab_id = lax.broadcasted_iota(jnp.int32, (RB, 128), 1).astype(F32)

    def forward(c, carry):
        drain(part_r.at[c], part_rs.at[c])
        enc8 = part[c, 0] + part_r[c, 0] + part_r[c, 1] + part_r[c, 2]
        for t in range(FT):
            cells = jnp.tanh(pred64[...] + enc8[t:t + 1, :])
            joint[pl.ds(pl.multiple_of(c * CELLS + t * LB, LB), LB), :] = cells.astype(BF16)
        base = pl.multiple_of(c * CELLS, CELLS)
        lg[...] = jnp.dot(joint[pl.ds(base, CELLS), :], w[...], preferred_element_type=F32)

        def soft(i, carry):
            at = pl.multiple_of(i * RB, RB)
            rows = pl.ds(at, RB)
            cell = pl.ds(pl.multiple_of(base + i * RB, RB), RB)
            tg = tgt64[pl.ds(pl.multiple_of((i % (LB // RB)) * RB, RB), RB), :]
            tiles = [lg[rows, n * 128:n * 128 + 128] for n in range(8)]
            m = tiles[0]
            for tile in tiles[1:]:
                m = jnp.maximum(m, tile)
            top = jnp.max(m, axis=1, keepdims=True)
            exps = [jnp.exp(tile - top) for tile in tiles]
            s = exps[0]
            for e in exps[1:]:
                s = s + e
            total = jnp.sum(s, axis=1, keepdims=True)
            scale = wsum[cell, :] / total
            lw = wlabel[cell, :]
            for n in range(8):
                g = exps[n] * scale - jnp.where(vocab_id == tg - float(n * 128), lw, 0.0)
                if n == 0:
                    g = g - jnp.where(vocab_id == 0.0, wblank[cell, :], 0.0)
                grad[cell, n * 128:n * 128 + 128] = g.astype(BF16)
            return carry

        lax.fori_loop(0, CELLS // RB, soft, 0, unroll=2)
        return carry

    lax.fori_loop(0, CH, forward, 0)

    def head_block(i):
        yy = (y + 1 + i) % 4
        col = pl.multiple_of(yy * 256, 256)
        block = lax.dot_general(
            grad[:, pl.ds(col, 256)], joint[...], (((0,), (0,)), ((), ())),
            preferred_element_type=F32,
        )
        for t in range(32):
            xl, zz, xh = t // 16, (t // 2) % 8, t % 2
            xx = xh * 2 + xl
            rows = block[t * 8:t * 8 + 8, :]
            hab[0, yy, 0, xx * 8 + zz] = rows[:, 0:128]
            hab[0, yy, 1, xx * 8 + zz] = rows[:, 128:256]
            hc[yy, zz * 4 + xx] = rows[:, 256:384]
            hab[1, yy, 0, xx * 8 + zz] = rows[:, 384:512]
            hab[1, yy, 1, xx * 8 + zz] = rows[:, 512:640]
        send(hab.at[1 - core, yy], h1ab.at[yy], h1ab_ss, h1ab_rs.at[yy], partner)

        @pl.when(core == 1)
        def _():
            send(hc.at[yy], h1c.at[yy], h1c_ss, h1c_rs.at[yy], partner)

    def head_spread(i):
        yy = (y + 1 + i) % 4
        drain(h1ab.at[yy], h1ab_rs.at[yy])
        hab[core, yy] = hab[core, yy] + h1ab[yy]
        for k in (1, 2, 3):
            at = pl.multiple_of(((x + k) % 4) * 8, 8)
            send(hab.at[core, yy, 0, pl.ds(at, 8)], p1a.at[k - 1, yy], p1_ss.at[0], p1_rs.at[0], x_peer(k))

        @pl.when(i < 3)
        def _():
            send(hab.at[core, yy, 1], p1b.at[i], p1_ss.at[1], p1_rs.at[1], {"frames": yy * 2 + x_lo})

        @pl.when(core == 0)
        def _():
            drain(h1c.at[yy], h1c_rs.at[yy])
            hc[yy] = hc[yy] + h1c[yy]
            for k in range(1, 8):
                at = pl.multiple_of(((z + k) % 8) * 4, 4)
                send(hc.at[yy, pl.ds(at, 4)], p1c.at[k - 1, yy], p1_ss.at[2], p1_rs.at[2], z_peer(k))

    def head_step(i, carry):
        head_block(i)

        @pl.when(i > 0)
        def _():
            head_spread(i - 1)

        return carry

    lax.fori_loop(0, 4, head_step, 0)

    predp[...] = jnp.zeros_like(predp)

    def backward(c, carry):
        base = pl.multiple_of(c * CELLS, CELLS)
        jg[...] = lax.dot_general(
            grad[pl.ds(base, CELLS), :], w[...], (((1,), (1,)), ((), ())), preferred_element_type=F32
        )
        for n in range(5):
            cols = slice(n * 128, n * 128 + 128)
            acc = predp[:, cols]
            for t in range(FT):
                cells = joint[pl.ds(pl.multiple_of(base + t * LB, LB), LB), cols].astype(F32)
                tg = jg[t * LB:t * LB + LB, cols] * (1.0 - cells * cells)
                acc = acc + tg
                encp[c * 2 + t // 4, t % 4:t % 4 + 1, cols] = jnp.sum(tg, axis=0, keepdims=True)
            predp[:, cols] = acc
        return carry

    backward(0, 0)
    head_spread(3)
    lax.fori_loop(1, CH, backward, 0)

    for k in range(1, 8):
        send(encp.at[(z + k) % 8], encp_r.at[k - 1], encp_ss, encp_rs, z_peer(k))
    for k in (1, 2, 3):
        send(predp.at[pl.ds(k * 16, 16)], predp_r.at[k - 1], predp_ss, predp_rs, h_peer(4 - k))

    drain(p1a, p1_rs.at[0])
    own = pl.ds(pl.multiple_of(x * 8, 8), 8)
    for yy in range(4):
        a1[yy] = hab[core, yy, 0, own] + p1a[0, yy] + p1a[1, yy] + p1a[2, yy]
    for k in (1, 2, 3):
        send(a1.at[(y + k) % 4], p2a.at[k - 1], p2_ss.at[0], p2_rs.at[0], y_peer(k))
    drain(p1b, p1_rs.at[1])
    b1[...] = hab[core, y, 1] + p1b[0] + p1b[1] + p1b[2]
    for k in (1, 2, 3):
        at = pl.multiple_of(((x + k) % 4) * 8, 8)
        send(b1.at[pl.ds(at, 8)], p2b.at[k - 1], p2_ss.at[1], p2_rs.at[1], x_peer(k))

    @pl.when(core == 0)
    def _():
        drain(p1c, p1_rs.at[2])
        mine = pl.ds(pl.multiple_of(z * 4, 4), 4)
        for yy in range(4):
            tot = hc[yy, mine]
            for k in range(7):
                tot = tot + p1c[k, yy]
            c1[yy] = tot
        for k in (1, 2, 3):
            send(c1.at[(y + k) % 4], p2c.at[k - 1], p2_ss.at[2], p2_rs.at[2], y_peer(k))

    drain(predp_r, predp_rs)
    predb[...] = predp[0:16, :] + predp_r[0] + predp_r[1] + predp_r[2]
    for k in range(1, 8):
        send(predb, predb_r.at[k - 1], predb_ss, predb_rs, f_peer(k))

    drain(p2a, p2_rs.at[0])
    a2 = a1[y] + p2a[0] + p2a[1] + p2a[2]
    drain(p2b, p2_rs.at[1])
    b2 = b1[own] + p2b[0] + p2b[1] + p2b[2]
    for zz in range(8):
        ab2[zz, 0] = a2[zz]
        ab2[zz, 1] = b2[zz]
    for k in range(1, 8):
        send(ab2.at[(z + k) % 8], p3ab.at[k - 1], p3_ss.at[0], p3_rs.at[0], z_peer(k))

    @pl.when(core == 0)
    def _():
        drain(p2c, p2_rs.at[2])
        c2[...] = c1[y] + p2c[0] + p2c[1] + p2c[2]
        for k in (1, 2, 3):
            send(c2.at[(x + k) % 4], p3c.at[k - 1], p3_ss.at[1], p3_rs.at[1], x_peer(k))

    drain(encp_r, encp_rs)
    tot = encp[z]
    for k in range(7):
        tot = tot + encp_r[k]
    enc_out[...] = tot

    drain(predb_r, predb_rs)
    tot = predb[...]
    for k in range(7):
        tot = tot + predb_r[k]
    pred_out[...] = tot

    drain(p3ab, p3_rs.at[0])
    tot = ab2[z]
    for k in range(7):
        tot = tot + p3ab[k]
    fin[core, 0:2] = tot

    @pl.when(core == 0)
    def _():
        drain(p3c, p3_rs.at[1])
        fin[0, 2] = c2[x] + p3c[0] + p3c[1] + p3c[2]
        send(fin.at[0], fin.at[0], fin_ss, fin_rs, partner)
        drain(fin.at[1, pl.ds(0, 2)], fin_rs)
        drain(fin.at[0], fin_ss)

    @pl.when(core == 1)
    def _():
        send(fin.at[1, pl.ds(0, 2)], fin.at[1, pl.ds(0, 2)], fin_ss, fin_rs, partner)
        drain(fin.at[0], fin_rs)
        drain(fin.at[1, pl.ds(0, 2)], fin_ss)

    for n in range(5):
        tile = fin[n // 3, n % 3]
        mine = jnp.where(core == 0, tile[0:4, :], tile[4:8, :])
        head_out[:, n * 128:n * 128 + 128] = mine * SCALE

    drain(msg_r, msg_ss)
    drain(part_r, part_ss)
    drain(encp_r, encp_ss)
    drain(predp_r, predp_ss)
    drain(predb_r, predb_ss)
    drain(h1ab, h1ab_ss)
    drain(p1a, p1_ss.at[0])
    drain(p1b, p1_ss.at[1])
    drain(p2a, p2_ss.at[0])
    drain(p2b, p2_ss.at[1])
    drain(p3ab, p3_ss.at[0])

    @pl.when(core == 0)
    def _():
        drain(p1c, p1_ss.at[2])
        drain(p2c, p2_ss.at[2])
        drain(p3c, p3_ss.at[1])

    @pl.when(core == 1)
    def _():
        drain(h1c, h1c_ss)


def on_device(features, up_weight, down_weight, predictor, out_weight, blank_weight, label_weight, targets):
    V = pltpu.VMEM
    dma = pltpu.SemaphoreType.DMA
    scratch = [
        V((128, 1024), BF16), V((1024, 1024), BF16), V((1024, JD), BF16), V((JD, VOCAB), BF16), dma((4,)),
        V((4, 16, JD + 128), F32), V((3, 16, JD + 128), F32), dma, dma,
        V((CH, 4, 8, JD), F32), V((CH, 3, 8, JD), F32), dma, dma((CH,)),
        V((LB, JD), F32), V((2048, 128), F32), V((2048, 128), F32), V((2048, 128), F32), V((LB, 128), F32),
        V((2048, JD), BF16), V((CELLS, VOCAB), F32), V((2048, VOCAB), BF16), V((CELLS, JD), F32),
        V((8, 4, JD), F32), V((7, 4, JD), F32), dma, dma,
        V((LB, JD), F32), V((3, 16, JD), F32), dma, dma,
        V((16, JD), F32), V((7, 16, JD), F32), dma, dma,
        V((2, 4, 2, 32, 8, 128), F32), V((4, 32, 8, 128), F32),
        V((4, 2, 32, 8, 128), F32), V((4, 32, 8, 128), F32), dma, dma((4,)), dma, dma((4,)),
        V((3, 4, 8, 8, 128), F32), V((3, 32, 8, 128), F32), V((7, 4, 4, 8, 128), F32), dma((3,)), dma((3,)),
        V((4, 8, 8, 128), F32), V((32, 8, 128), F32), V((4, 4, 8, 128), F32),
        V((3, 8, 8, 128), F32), V((3, 8, 8, 128), F32), V((3, 4, 8, 128), F32), dma((3,)), dma((3,)),
        V((8, 2, 8, 128), F32), V((4, 8, 128), F32), V((7, 2, 8, 128), F32), V((3, 8, 128), F32),
        dma((2,)), dma((2,)),
        V((2, 3, 8, 128), F32), dma, dma,
    ]
    hbm = pl.BlockSpec(memory_space=pl.ANY)
    vmem = pl.BlockSpec(memory_space=pltpu.VMEM)
    smem = pl.BlockSpec(memory_space=pltpu.SMEM)
    return pl.pallas_call(
        kernel,
        out_shape=(
            jax.ShapeDtypeStruct((4, JD), F32),
            jax.ShapeDtypeStruct((16, JD), F32),
            jax.ShapeDtypeStruct((4, JD), F32),
        ),
        in_specs=[hbm, hbm, hbm, vmem, hbm, vmem, vmem, smem],
        out_specs=(vmem, vmem, vmem),
        scratch_shapes=scratch,
        compiler_params=pltpu.CompilerParams(
            collective_id=0, has_side_effects=True, vmem_limit_bytes=60 * 1024 * 1024
        ),
    )(features, up_weight, down_weight, predictor, out_weight, blank_weight, label_weight, targets)


def solution(mesh):
    placed = (
        P("frames", None),
        P(None, "hidden"),
        P("hidden", None),
        P(("labels", "hidden"), None),
        P(),
        P("frames", ("labels", "hidden")),
        P("frames", ("labels", "hidden")),
        P(("labels", "hidden")),
    )
    return jax.shard_map(
        on_device,
        mesh=mesh,
        in_specs=placed,
        out_specs=(
            P(("frames", "labels", "hidden"), None),
            P(("labels", "hidden"), None),
            P(("frames", "labels", "hidden"), None),
        ),
        check_vma=False,
    )
```

```python
import math

import jax
import jax.numpy as jnp
from jax import lax
from jax.experimental import pallas as pl
from jax.experimental.pallas import tpu as pltpu
from jax.sharding import PartitionSpec as P

F32 = jnp.float32
BF16 = jnp.bfloat16
JD = 640
VOCAB = 1024
CH = 4
FT = 8
LB = 64
CELLS = FT * LB
RB = 16
SCALE = 1.0 / math.sqrt(1024 * 512)


def send(src, dst, send_sem, recv_sem, device):
    pltpu.make_async_remote_copy(
        src_ref=src,
        dst_ref=dst,
        send_sem=send_sem,
        recv_sem=recv_sem,
        device_id=device,
        device_id_type=pl.DeviceIdType.MESH,
    ).start()


def drain(ref, sem):
    pltpu.make_async_copy(ref, ref, sem).wait()


def kernel(
    feat_hbm, up_hbm, down_hbm, pred_hbm, w_hbm, blank_hbm, label_hbm, targets,
    enc_out, pred_out, head_out,
    feat, up, down, w, pred_in, blank_in, label_in, load_sem,
    msg, msg_r, msg_ss, msg_rs,
    part, part_r, part_ss, part_rs,
    pred64, wsum, wblank, wlabel, hot,
    joint, lg, grad, jg,
    encp, encp_r, encp_ss, encp_rs,
    predp, predp_r, predp_ss, predp_rs,
    predb, predb_r, predb_ss, predb_rs,
    hab, hc, h1ab, h1c, h1ab_ss, h1ab_rs, h1c_ss, h1c_rs,
    p1a, p1b, p1c, p1_ss, p1_rs,
    a1, b1, c1, p2a, p2b, p2c, p2_ss, p2_rs,
    ab2, c2, p3own, p3oth, p3c, p3d, p3_ss, p3_rs,
    fin,
):
    f = lax.axis_index("frames")
    z = lax.axis_index("labels")
    h = lax.axis_index("hidden")
    y, x_lo = f // 2, f % 2
    x_hi, core = h // 2, h % 2
    x = x_hi * 2 + x_lo

    def h_peer(k):
        return {"hidden": (h + k) % 4}

    def z_peer(k):
        return {"labels": (z + k) % 8}

    def y_peer(k):
        return {"frames": ((y + k) % 4) * 2 + x_lo}

    def x_peer(k):
        xx = (x + k) % 4
        return {"frames": y * 2 + xx % 2, "hidden": (xx // 2) * 2 + core}

    def f_peer(k):
        return {"frames": (f + k) % 8}

    other = x_hi * 2 + (1 - core)
    partner = {"hidden": other}

    def z_other(k):
        return {"labels": (z + k) % 8, "hidden": other}

    def x_other(k):
        xx = (x + k) % 4
        return {"frames": y * 2 + xx % 2, "hidden": (xx // 2) * 2 + (1 - core)}

    barrier = pltpu.get_barrier_semaphore()
    greeted = [h_peer(k) for k in (1, 2, 3)] + [z_peer(k) for k in range(1, 8)]
    greeted += [f_peer(k) for k in range(1, 8)] + [x_peer(k) for k in (1, 3)]
    greeted += [z_other(k) for k in range(1, 8)] + [x_other(k) for k in (1, 3)]
    for device in greeted:
        pl.semaphore_signal(barrier, inc=1, device_id=device, device_id_type=pl.DeviceIdType.MESH)

    pairs = (
        (feat_hbm, feat), (blank_hbm, blank_in), (label_hbm, label_in), (pred_hbm, pred_in),
        (up_hbm, up), (down_hbm, down), (w_hbm, w),
    )
    loads = [pltpu.make_async_copy(a, b, load_sem.at[n]) for n, (a, b) in enumerate(pairs)]
    for load in loads:
        load.start()

    prow = lax.broadcasted_iota(jnp.int32, (128, 128), 0)
    pcol = lax.broadcasted_iota(jnp.int32, (128, 128), 1)
    pr = prow % 8
    pframe = ((prow // 32) * 2 + pr // 4) * 16 + ((h + (prow // 8) % 4) % 4) * 4 + pr % 4
    perm = (pcol == pframe).astype(F32).astype(BF16)
    tcol = jnp.zeros((16, 128), jnp.int32)
    trow = lax.broadcasted_iota(jnp.int32, (16, 128), 0)
    for i in range(16):
        tcol = jnp.where(trow == i, targets[i], tcol)
    tfloat = tcol.astype(F32)
    lane = lax.broadcasted_iota(jnp.int32, (16, 128), 1) % 16
    for n in range(4):
        loads[n].wait()
    feat_p = jnp.dot(perm, feat[...], preferred_element_type=F32).astype(BF16)

    pred_wide = pred_in[...].astype(F32)
    for d in range(4):
        msg[d, :, 0:JD] = pred_wide
        b = pltpu.roll(blank_in[...], (128 - 4 * d) % 128, 1)
        l = pltpu.roll(label_in[...], (132 - 4 * d) % 128, 1)
        msg[d, :, JD:JD + 128] = jnp.where(lane < 4, b, jnp.where(lane < 8, l, tfloat))

    loads[4].wait()
    hidden = jnp.maximum(jnp.dot(feat_p, up[...], preferred_element_type=F32), 0.0).astype(BF16)

    pl.semaphore_wait(barrier, len(greeted))
    for k in (1, 2, 3):
        send(msg.at[(h + k) % 4], msg_r.at[k - 1], msg_ss, msg_rs, h_peer(k))

    loads[5].wait()
    enc = jnp.dot(hidden, down[...], preferred_element_type=F32)
    for c in range(CH):
        for k in range(4):
            r = c * 32 + k * 8
            part[c, k] = enc[r:r + 8, :]
    for c in range(CH):
        for k in (1, 2, 3):
            send(part.at[c, k], part_r.at[c, k - 1], part_ss, part_rs.at[c], h_peer(k))

    vocab_id = lax.broadcasted_iota(jnp.int32, (RB, 128), 1).astype(F32)
    drain(msg_r, msg_rs)
    for k in range(4):
        src = msg.at[h] if k == 0 else msg_r.at[k - 1]
        rows = slice(k * 16, k * 16 + 16)
        pred64[rows, :] = src[:, 0:JD]
        tail = src[:, JD:JD + 128]
        tg = jnp.broadcast_to(tail[:, 8:9], (16, 128))
        for n in range(8):
            hot[rows, n * 128:n * 128 + 128] = jnp.where(vocab_id == tg - float(n * 128), 1.0, 0.0)
        for t in range(CH * FT):
            r = t * LB + k * 16
            at = (t // 4) * 16 + t % 4
            b = jnp.broadcast_to(tail[:, at:at + 1], (16, 128))
            l = jnp.broadcast_to(tail[:, at + 4:at + 5], (16, 128))
            wsum[r:r + 16, :] = b + l
            wblank[r:r + 16, :] = b
            wlabel[r:r + 16, :] = l
    loads[6].wait()

    def logits_of(c):
        drain(part_r.at[c], part_rs.at[c])
        enc8 = part[c, 0] + part_r[c, 0] + part_r[c, 1] + part_r[c, 2]
        for t in range(FT):
            cells = jnp.tanh(pred64[...] + enc8[t:t + 1, :])
            joint[c * CELLS + t * LB:c * CELLS + t * LB + LB, :] = cells.astype(BF16)
        lg[c % 2] = jnp.dot(joint[c * CELLS:c * CELLS + CELLS, :], w[...], preferred_element_type=F32)

    def softmax_of(c):
        for i in range(CELLS // RB):
            rows = slice(i * RB, i * RB + RB)
            cell = slice(c * CELLS + i * RB, c * CELLS + i * RB + RB)
            label = slice((i * RB) % LB, (i * RB) % LB + RB)
            tiles = [lg[c % 2, rows, n * 128:n * 128 + 128] for n in range(8)]
            m = tiles[0]
            for tile in tiles[1:]:
                m = jnp.maximum(m, tile)
            top = jnp.max(m, axis=1, keepdims=True)
            exps = [jnp.exp(tile - top) for tile in tiles]
            s = exps[0]
            for e in exps[1:]:
                s = s + e
            scale = wsum[cell, :] / jnp.sum(s, axis=1, keepdims=True)
            lw = wlabel[cell, :]
            for n in range(8):
                g = exps[n] * scale - lw * hot[label, n * 128:n * 128 + 128]
                if n == 0:
                    g = g - jnp.where(vocab_id == 0.0, wblank[cell, :], 0.0)
                grad[cell, n * 128:n * 128 + 128] = g.astype(BF16)

    logits_of(0)
    for c in range(1, CH):
        logits_of(c)
        softmax_of(c - 1)
    softmax_of(CH - 1)

    def head_block(i):
        yy = (y + 1 + i) % 4
        col = pl.multiple_of(yy * 256, 256)
        block = lax.dot_general(
            grad[:, pl.ds(col, 256)], joint[...], (((0,), (0,)), ((), ())),
            preferred_element_type=F32,
        )
        for t in range(32):
            xl, zz, xh = t // 16, (t // 2) % 8, t % 2
            xx = xh * 2 + xl
            rows = block[t * 8:t * 8 + 8, :]
            hab[0, yy, 0, xx * 8 + zz] = rows[:, 0:128]
            hab[0, yy, 1, xx * 8 + zz] = rows[:, 128:256]
            hc[yy, zz * 4 + xx] = rows[:, 256:384]
            hab[1, yy, 0, xx * 8 + zz] = rows[:, 384:512]
            hab[1, yy, 1, xx * 8 + zz] = rows[:, 512:640]
        send(hab.at[1 - core, yy], h1ab.at[yy], h1ab_ss, h1ab_rs.at[yy], partner)

        @pl.when(core == 1)
        def _():
            send(hc.at[yy], h1c.at[yy], h1c_ss, h1c_rs.at[yy], partner)

    def head_spread(i):
        yy = (y + 1 + i) % 4
        drain(h1ab.at[yy], h1ab_rs.at[yy])
        hab[core, yy] = hab[core, yy] + h1ab[yy]
        for k in (1, 2, 3):
            at = pl.multiple_of(((x + k) % 4) * 8, 8)
            send(hab.at[core, yy, 0, pl.ds(at, 8)], p1a.at[k - 1, yy], p1_ss.at[0], p1_rs.at[0], x_peer(k))

        @pl.when(i < 3)
        def _():
            send(hab.at[core, yy, 1], p1b.at[i], p1_ss.at[1], p1_rs.at[1], {"frames": yy * 2 + x_lo})

        @pl.when(core == 0)
        def _():
            drain(h1c.at[yy], h1c_rs.at[yy])
            hc[yy] = hc[yy] + h1c[yy]
            for k in range(1, 8):
                at = pl.multiple_of(((z + k) % 8) * 4, 4)
                send(hc.at[yy, pl.ds(at, 4)], p1c.at[k - 1, yy], p1_ss.at[2], p1_rs.at[2], z_peer(k))

    def head_step(i, carry):
        head_block(i)

        @pl.when(i > 0)
        def _():
            head_spread(i - 1)

        return carry

    lax.fori_loop(0, 4, head_step, 0)

    predp[...] = jnp.zeros_like(predp)

    def backward(c, carry):
        base = pl.multiple_of(c * CELLS, CELLS)
        jg[...] = lax.dot_general(
            grad[pl.ds(base, CELLS), :], w[...], (((1,), (1,)), ((), ())), preferred_element_type=F32
        )
        for n in range(5):
            cols = slice(n * 128, n * 128 + 128)
            acc = predp[:, cols]
            for t in range(FT):
                cells = joint[pl.ds(pl.multiple_of(base + t * LB, LB), LB), cols].astype(F32)
                tg = jg[t * LB:t * LB + LB, cols] * (1.0 - cells * cells)
                acc = acc + tg
                encp[c * 2 + t // 4, t % 4:t % 4 + 1, cols] = jnp.sum(tg, axis=0, keepdims=True)
            predp[:, cols] = acc
        return carry

    backward(0, 0)
    head_spread(3)
    lax.fori_loop(1, CH, backward, 0)

    for k in range(1, 8):
        send(encp.at[(z + k) % 8], encp_r.at[k - 1], encp_ss, encp_rs, z_peer(k))
    for k in (1, 2, 3):
        send(predp.at[pl.ds(k * 16, 16)], predp_r.at[k - 1], predp_ss, predp_rs, h_peer(4 - k))

    drain(p1a, p1_rs.at[0])
    own = pl.ds(pl.multiple_of(x * 8, 8), 8)
    for yy in range(4):
        a1[yy] = hab[core, yy, 0, own] + p1a[0, yy] + p1a[1, yy] + p1a[2, yy]
    for k in (1, 2, 3):
        send(a1.at[(y + k) % 4], p2a.at[k - 1], p2_ss.at[0], p2_rs.at[0], y_peer(k))
    drain(p1b, p1_rs.at[1])
    b1[...] = hab[core, y, 1] + p1b[0] + p1b[1] + p1b[2]
    for k in (1, 2, 3):
        at = pl.multiple_of(((x + k) % 4) * 8, 8)
        send(b1.at[pl.ds(at, 8)], p2b.at[k - 1], p2_ss.at[1], p2_rs.at[1], x_peer(k))

    @pl.when(core == 0)
    def _():
        drain(p1c, p1_rs.at[2])
        mine = pl.ds(pl.multiple_of(z * 4, 4), 4)
        for yy in range(4):
            tot = hc[yy, mine]
            for k in range(7):
                tot = tot + p1c[k, yy]
            c1[yy] = tot
        for k in (1, 2, 3):
            send(c1.at[(y + k) % 4], p2c.at[k - 1], p2_ss.at[2], p2_rs.at[2], y_peer(k))

    drain(predp_r, predp_rs)
    predb[...] = predp[0:16, :] + predp_r[0] + predp_r[1] + predp_r[2]
    for k in range(1, 8):
        send(predb, predb_r.at[k - 1], predb_ss, predb_rs, f_peer(k))

    drain(p2a, p2_rs.at[0])
    a2 = a1[y] + p2a[0] + p2a[1] + p2a[2]
    drain(p2b, p2_rs.at[1])
    b2 = b1[own] + p2b[0] + p2b[1] + p2b[2]
    for zz in range(8):
        ab2[zz, 0] = a2[zz]
        ab2[zz, 1] = b2[zz]
    for k in range(8):
        send(ab2.at[(z + k) % 8], p3oth.at[k], p3_ss.at[1], p3_rs.at[1], z_other(k))
        if k:
            send(ab2.at[(z + k) % 8], p3own.at[k - 1], p3_ss.at[0], p3_rs.at[0], z_peer(k))

    @pl.when(core == 0)
    def _():
        drain(p2c, p2_rs.at[2])
        c2[...] = c1[y] + p2c[0] + p2c[1] + p2c[2]
        for k in range(4):
            send(c2.at[(x + k) % 4], p3d.at[k], p3_ss.at[3], p3_rs.at[3], x_other(k))
            if k:
                send(c2.at[(x + k) % 4], p3c.at[k - 1], p3_ss.at[2], p3_rs.at[2], x_peer(k))

    drain(encp_r, encp_rs)
    tot = encp[z]
    for k in range(7):
        tot = tot + encp_r[k]
    enc_out[...] = tot

    drain(predb_r, predb_rs)
    tot = predb[...]
    for k in range(7):
        tot = tot + predb_r[k]
    pred_out[...] = tot

    drain(p3own, p3_rs.at[0])
    tot = ab2[z]
    for k in range(7):
        tot = tot + p3own[k]
    fin[core, 0:2] = tot
    drain(p3oth, p3_rs.at[1])
    tot = p3oth[0]
    for k in range(1, 8):
        tot = tot + p3oth[k]
    fin[1 - core, 0:2] = tot

    @pl.when(core == 0)
    def _():
        drain(p3c, p3_rs.at[2])
        fin[0, 2] = c2[x] + p3c[0] + p3c[1] + p3c[2]

    @pl.when(core == 1)
    def _():
        drain(p3d, p3_rs.at[3])
        fin[0, 2] = p3d[0] + p3d[1] + p3d[2] + p3d[3]

    for n in range(5):
        tile = fin[n // 3, n % 3]
        mine = jnp.where(core == 0, tile[0:4, :], tile[4:8, :])
        head_out[:, n * 128:n * 128 + 128] = mine

    drain(msg_r, msg_ss)
    drain(part_r, part_ss)
    drain(encp_r, encp_ss)
    drain(predp_r, predp_ss)
    drain(predb_r, predb_ss)
    drain(h1ab, h1ab_ss)
    drain(p1a, p1_ss.at[0])
    drain(p1b, p1_ss.at[1])
    drain(p2a, p2_ss.at[0])
    drain(p2b, p2_ss.at[1])
    drain(p3own, p3_ss.at[0])
    drain(p3oth, p3_ss.at[1])

    @pl.when(core == 0)
    def _():
        drain(p1c, p1_ss.at[2])
        drain(p2c, p2_ss.at[2])
        drain(p3c, p3_ss.at[2])
        drain(p3d, p3_ss.at[3])

    @pl.when(core == 1)
    def _():
        drain(h1c, h1c_ss)


def hand_on(enc_in, pred_in, head_in, enc_out, pred_out, head_out):
    enc_out[...] = enc_in[...]
    pred_out[...] = pred_in[...]
    head_out[...] = head_in[...] * SCALE


def on_device(features, up_weight, down_weight, predictor, out_weight, blank_weight, label_weight, targets):
    V = pltpu.VMEM
    dma = pltpu.SemaphoreType.DMA
    scratch = [
        V((128, 1024), BF16), V((1024, 1024), BF16), V((1024, JD), BF16), V((JD, VOCAB), BF16),
        V((16, JD), BF16), V((16, 128), F32), V((16, 128), F32), dma((7,)),
        V((4, 16, JD + 128), F32), V((3, 16, JD + 128), F32), dma, dma,
        V((CH, 4, 8, JD), F32), V((CH, 3, 8, JD), F32), dma, dma((CH,)),
        V((LB, JD), F32), V((2048, 128), F32), V((2048, 128), F32), V((2048, 128), F32), V((LB, VOCAB), F32),
        V((2048, JD), BF16), V((2, CELLS, VOCAB), F32), V((2048, VOCAB), BF16), V((CELLS, JD), F32),
        V((8, 4, JD), F32), V((7, 4, JD), F32), dma, dma,
        V((LB, JD), F32), V((3, 16, JD), F32), dma, dma,
        V((16, JD), F32), V((7, 16, JD), F32), dma, dma,
        V((2, 4, 2, 32, 8, 128), F32), V((4, 32, 8, 128), F32),
        V((4, 2, 32, 8, 128), F32), V((4, 32, 8, 128), F32), dma, dma((4,)), dma, dma((4,)),
        V((3, 4, 8, 8, 128), F32), V((3, 32, 8, 128), F32), V((7, 4, 4, 8, 128), F32), dma((3,)), dma((3,)),
        V((4, 8, 8, 128), F32), V((32, 8, 128), F32), V((4, 4, 8, 128), F32),
        V((3, 8, 8, 128), F32), V((3, 8, 8, 128), F32), V((3, 4, 8, 128), F32), dma((3,)), dma((3,)),
        V((8, 2, 8, 128), F32), V((4, 8, 128), F32), V((7, 2, 8, 128), F32), V((8, 2, 8, 128), F32),
        V((3, 8, 128), F32), V((4, 8, 128), F32), dma((4,)), dma((4,)),
        V((2, 3, 8, 128), F32),
    ]
    hbm = pl.BlockSpec(memory_space=pl.ANY)
    vmem = pl.BlockSpec(memory_space=pltpu.VMEM)
    smem = pl.BlockSpec(memory_space=pltpu.SMEM)
    shapes = (
        jax.ShapeDtypeStruct((4, JD), F32),
        jax.ShapeDtypeStruct((16, JD), F32),
        jax.ShapeDtypeStruct((4, JD), F32),
    )
    results = pl.pallas_call(
        kernel,
        out_shape=shapes,
        in_specs=[hbm] * 7 + [smem],
        out_specs=(vmem, vmem, vmem),
        scratch_shapes=scratch,
        compiler_params=pltpu.CompilerParams(
            collective_id=0, has_side_effects=True, vmem_limit_bytes=60 * 1024 * 1024
        ),
    )(features, up_weight, down_weight, predictor, out_weight, blank_weight.T, label_weight.T, targets)
    return pl.pallas_call(
        hand_on, out_shape=shapes, in_specs=[vmem] * 3, out_specs=(vmem,) * 3
    )(*results)


def solution(mesh):
    placed = (
        P("frames", None),
        P(None, "hidden"),
        P("hidden", None),
        P(("labels", "hidden"), None),
        P(),
        P("frames", ("labels", "hidden")),
        P("frames", ("labels", "hidden")),
        P(("labels", "hidden")),
    )
    return jax.shard_map(
        on_device,
        mesh=mesh,
        in_specs=placed,
        out_specs=(
            P(("frames", "labels", "hidden"), None),
            P(("labels", "hidden"), None),
            P(("frames", "labels", "hidden"), None),
        ),
        check_vma=False,
    )
```

```python
import math

import jax
import jax.numpy as jnp
from jax import lax
from jax.experimental import pallas as pl
from jax.experimental.pallas import tpu as pltpu
from jax.sharding import PartitionSpec as P

F32 = jnp.float32
BF16 = jnp.bfloat16
JD = 640
VOCAB = 1024
FR = 32
LB = 64
CH = 4
FT = FR // CH
CELLS = FT * LB
RB = 16
SCALE = 1.0 / math.sqrt(1024 * 512)


def send(src, dst, send_sem, recv_sem, device):
    pltpu.make_async_remote_copy(
        src_ref=src,
        dst_ref=dst,
        send_sem=send_sem,
        recv_sem=recv_sem,
        device_id=device,
        device_id_type=pl.DeviceIdType.MESH,
    ).start()


def drain(ref, sem):
    pltpu.make_async_copy(ref, ref, sem).wait()


def kernel(
    feat_hbm, up_hbm, down_hbm, pred_hbm, w_hbm, blank_hbm, label_hbm, targets,
    enc_out, pred_out, head_out,
    feat, up, down, w, pred_in, blank_in, label_in, load_sem,
    msg, msg_r, msg_ss, msg_rs,
    part, part_r, part_ss, part_rs,
    pred64, wsum, wblank, wlabel, hot, encacc,
    joint, lg, grad, jg,
    encp, encp_r, encp_ss, encp_rs,
    predp, predp_r, predp_ss, predp_rs,
    predb, predb_r, predb_ss, predb_rs,
    hab, hc, h1ab, h1c, h1ab_ss, h1ab_rs, h1c_ss, h1c_rs,
    p1a, p1b, p1c, p1_ss, p1a_rs, p1b_rs, p1c_rs,
    a1, b1, c1, p2a, p2b, p2c, p2_ss, p2_rs,
    ab2, c2, p3own, p3oth, p3c, p3d, p3_ss, p3_rs,
    fin,
):
    f = lax.axis_index("frames")
    z = lax.axis_index("labels")
    h = lax.axis_index("hidden")
    y, x_lo = f // 2, f % 2
    x_hi, core = h // 2, h % 2
    x = x_hi * 2 + x_lo

    def h_of(s):
        return ((x_hi + s // 2) % 2) * 2 + (core + s % 2) % 2

    def h_peer(s):
        return {"hidden": h_of(s)}

    def z_peer(k):
        return {"labels": (z + k) % 8}

    def y_peer(k):
        return {"frames": ((y + k) % 4) * 2 + x_lo}

    def x_peer(k):
        xx = (x + k) % 4
        return {"frames": y * 2 + xx % 2, "hidden": (xx // 2) * 2 + core}

    def f_peer(k):
        return {"frames": (f + k) % 8}

    other = x_hi * 2 + (1 - core)
    partner = {"hidden": other}

    def z_other(k):
        return {"labels": (z + k) % 8, "hidden": other}

    def x_other(k):
        xx = (x + k) % 4
        return {"frames": y * 2 + xx % 2, "hidden": (xx // 2) * 2 + (1 - core)}

    barrier = pltpu.get_barrier_semaphore()
    greeted = [h_peer(s) for s in (1, 2, 3)] + [z_peer(k) for k in range(1, 8)]
    greeted += [f_peer(k) for k in range(1, 8)] + [x_peer(k) for k in (1, 3)]
    greeted += [z_other(k) for k in range(1, 8)] + [x_other(k) for k in (1, 3)]
    for device in greeted:
        pl.semaphore_signal(barrier, inc=1, device_id=device, device_id_type=pl.DeviceIdType.MESH)

    pairs = (
        (feat_hbm, feat), (blank_hbm, blank_in), (label_hbm, label_in), (pred_hbm, pred_in),
        (up_hbm, up), (down_hbm, down), (w_hbm, w),
    )
    loads = [pltpu.make_async_copy(a, b, load_sem.at[n]) for n, (a, b) in enumerate(pairs)]
    for load in loads:
        load.start()

    prow = lax.broadcasted_iota(jnp.int32, (128, 128), 0)
    pcol = lax.broadcasted_iota(jnp.int32, (128, 128), 1)
    pslot = (prow // 8) % 4
    pj = (prow // 32) * 8 + prow % 8
    pframe = (pj // 4) * 16 + h_of(pslot) * 4 + pj % 4
    perm = (pcol == pframe).astype(F32).astype(BF16)
    tcol = jnp.zeros((16, 128), jnp.int32)
    trow = lax.broadcasted_iota(jnp.int32, (16, 128), 0)
    for i in range(16):
        tcol = jnp.where(trow == i, targets[i], tcol)
    tfloat = tcol.astype(F32)
    lane = lax.broadcasted_iota(jnp.int32, (16, 128), 1) % 16
    for n in range(4):
        loads[n].wait()
    feat_p = jnp.dot(perm, feat[...], preferred_element_type=F32).astype(BF16)

    pred_wide = pred_in[...].astype(F32)
    for d in range(4):
        msg[d, :, 0:JD] = pred_wide
        b = pltpu.roll(blank_in[...], (128 - 4 * d) % 128, 1)
        l = pltpu.roll(label_in[...], (132 - 4 * d) % 128, 1)
        msg[d, :, JD:JD + 128] = jnp.where(lane < 4, b, jnp.where(lane < 8, l, tfloat))

    loads[4].wait()
    hidden = jnp.maximum(jnp.dot(feat_p, up[...], preferred_element_type=F32), 0.0).astype(BF16)

    loads[5].wait()
    enc = jnp.dot(hidden, down[...], preferred_element_type=F32)
    for c in range(CH):
        for s in range(4):
            r = c * 32 + s * 8
            part[c, s] = enc[r:r + 8, :]
    vocab_id = lax.broadcasted_iota(jnp.int32, (RB, 128), 1).astype(F32)

    def labels_of(k):
        if k:
            drain(msg_r.at[k - 1], msg_rs.at[k - 1])
        src = msg_r.at[k - 1] if k else msg.at[h]
        rows = slice(k * 16, k * 16 + 16)
        pred64[rows, :] = src[:, 0:JD]
        tail = src[:, JD:JD + 128]
        tg = jnp.broadcast_to(tail[:, 8:9], (16, 128))
        for n in range(8):
            hot[rows, n * 128:n * 128 + 128] = jnp.where(vocab_id == tg - float(n * 128), 1.0, 0.0)
        for t in range(FR):
            r = (k * FR + t) * 16
            at = (t // 4) * 16 + t % 4
            b = jnp.broadcast_to(tail[:, at:at + 1], (16, 128))
            l = jnp.broadcast_to(tail[:, at + 4:at + 5], (16, 128))
            wsum[r:r + 16, :] = b + l
            wblank[r:r + 16, :] = b
            wlabel[r:r + 16, :] = l

    labels_of(0)
    pl.semaphore_wait(barrier, len(greeted))
    for s in (2, 3, 1):
        send(msg.at[h_of(s)], msg_r.at[s - 1], msg_ss, msg_rs.at[s - 1], h_peer(s))
    for c in range(CH):
        for s in (2, 3, 1):
            send(part.at[c, s], part_r.at[c, s - 1], part_ss, part_rs.at[c], h_peer(s))
    for k in (1, 2, 3):
        labels_of(k)
    loads[6].wait()

    def logits_of(c):
        drain(part_r.at[c], part_rs.at[c])
        enc8 = part[c, 0] + part_r[c, 0] + part_r[c, 1] + part_r[c, 2]
        for t in range(FT):
            cells = jnp.tanh(pred64[...] + enc8[t:t + 1, :]).astype(BF16)
            for k in range(4):
                r = (k * FR + c * FT + t) * 16
                joint[r:r + 16, :] = cells[k * 16:k * 16 + 16, :]
        ends = [(k * FR + c * FT) * 16 for k in range(4)]
        lhs = jnp.concatenate([joint[r:r + FT * 16, :] for r in ends], axis=0)
        lg[c % 2] = jnp.dot(lhs, w[...], preferred_element_type=F32)

    def softmax_of(c):
        for i in range(CELLS // RB):
            rows = slice(i * RB, i * RB + RB)
            block, t = i // FT, c * FT + i % FT
            r = (block * FR + t) * 16
            cell = slice(r, r + 16)
            label = slice(block * 16, block * 16 + 16)
            tiles = [lg[c % 2, rows, n * 128:n * 128 + 128] for n in range(8)]
            m = tiles[0]
            for tile in tiles[1:]:
                m = jnp.maximum(m, tile)
            top = jnp.max(m, axis=1, keepdims=True)
            exps = [jnp.exp(tile - top) for tile in tiles]
            s = exps[0]
            for e in exps[1:]:
                s = s + e
            scale = wsum[cell, :] / jnp.sum(s, axis=1, keepdims=True)
            lw = wlabel[cell, :]
            for n in range(8):
                g = exps[n] * scale - lw * hot[label, n * 128:n * 128 + 128]
                if n == 0:
                    g = g - jnp.where(vocab_id == 0.0, wblank[cell, :], 0.0)
                grad[cell, n * 128:n * 128 + 128] = g.astype(BF16)

    logits_of(0)
    for c in range(1, 4):
        logits_of(c)
        softmax_of(c - 1)
    softmax_of(3)

    def head_block(i):
        yy = (y + 1 + i) % 4
        col = pl.multiple_of(yy * 256, 256)
        block = lax.dot_general(
            grad[:, pl.ds(col, 256)], joint[...], (((0,), (0,)), ((), ())),
            preferred_element_type=F32,
        )
        for t in range(32):
            xl, zz, xh = t // 16, (t // 2) % 8, t % 2
            xx = xh * 2 + xl
            rows = block[t * 8:t * 8 + 8, :]
            hab[0, yy, 0, xx * 8 + zz] = rows[:, 0:128]
            hab[0, yy, 1, xx * 8 + zz] = rows[:, 128:256]
            hc[yy, zz * 4 + xx] = rows[:, 256:384]
            hab[1, yy, 0, xx * 8 + zz] = rows[:, 384:512]
            hab[1, yy, 1, xx * 8 + zz] = rows[:, 512:640]
        send(hab.at[1 - core, yy], h1ab.at[yy], h1ab_ss, h1ab_rs.at[yy], partner)

        @pl.when(core == 1)
        def _():
            send(hc.at[yy], h1c.at[yy], h1c_ss, h1c_rs.at[yy], partner)

    def head_spread(i):
        yy = (y + 1 + i) % 4
        drain(h1ab.at[yy], h1ab_rs.at[yy])
        hab[core, yy] = hab[core, yy] + h1ab[yy]
        for k in (1, 2, 3):
            at = pl.multiple_of(((x + k) % 4) * 8, 8)
            send(hab.at[core, yy, 0, pl.ds(at, 8)], p1a.at[yy, k - 1], p1_ss.at[0], p1a_rs.at[yy], x_peer(k))

        @pl.when(i < 3)
        def _():
            send(hab.at[core, yy, 1], p1b.at[i], p1_ss.at[1], p1b_rs, {"frames": yy * 2 + x_lo})

        @pl.when(core == 0)
        def _():
            drain(h1c.at[yy], h1c_rs.at[yy])
            hc[yy] = hc[yy] + h1c[yy]
            for k in range(1, 8):
                at = pl.multiple_of(((z + k) % 8) * 4, 4)
                send(hc.at[yy, pl.ds(at, 4)], p1c.at[yy, k - 1], p1_ss.at[2], p1c_rs.at[yy], z_peer(k))

    own = pl.ds(pl.multiple_of(x * 8, 8), 8)
    mine = pl.ds(pl.multiple_of(z * 4, 4), 4)

    def second_a(i, away=True):
        yy = (y + 1 + i) % 4
        drain(p1a.at[yy], p1a_rs.at[yy])
        a1[yy] = hab[core, yy, 0, own] + p1a[yy, 0] + p1a[yy, 1] + p1a[yy, 2]
        if away:
            send(a1.at[yy], p2a.at[i], p2_ss.at[0], p2_rs.at[0], {"frames": yy * 2 + x_lo})

    def second_b():
        drain(p1b, p1b_rs)
        b1[...] = hab[core, y, 1] + p1b[0] + p1b[1] + p1b[2]
        for k in (1, 2, 3):
            at = pl.multiple_of(((x + k) % 4) * 8, 8)
            send(b1.at[pl.ds(at, 8)], p2b.at[k - 1], p2_ss.at[1], p2_rs.at[1], x_peer(k))

    def second_c(i, away=True):
        @pl.when(core == 0)
        def _():
            yy = (y + 1 + i) % 4
            drain(p1c.at[yy], p1c_rs.at[yy])
            tot = hc[yy, mine]
            for k in range(7):
                tot = tot + p1c[yy, k]
            c1[yy] = tot
            if away:
                send(c1.at[yy], p2c.at[i], p2_ss.at[2], p2_rs.at[2], {"frames": yy * 2 + x_lo})

    def head_step(i, carry):
        head_block(i)

        @pl.when(i > 0)
        def _():
            head_spread(i - 1)

        return carry

    lax.fori_loop(0, 4, head_step, 0)

    def backward(k, first=False, last=False):
        r = k * FR * 16
        jg[...] = lax.dot_general(
            grad[r:r + FR * 16, :], w[...], (((1,), (1,)), ((), ())), preferred_element_type=F32
        )
        for n in range(5):
            cols = slice(n * 128, n * 128 + 128)
            acc = jnp.zeros((16, 128), F32)
            for t in range(FR):
                cells = joint[r + t * 16:r + t * 16 + 16, cols].astype(F32)
                tg = jg[t * 16:t * 16 + 16, cols] * (1.0 - cells * cells)
                acc = acc + tg
                both = tg[0:8, :] + tg[8:16, :]
                if not first:
                    both = both + encacc[t, :, cols]
                if last:
                    encp[t // 4, t % 4:t % 4 + 1, cols] = jnp.sum(both, axis=0, keepdims=True)
                else:
                    encacc[t, :, cols] = both
            predp[k * 16:k * 16 + 16, cols] = acc
        if k:
            send(predp.at[pl.ds(k * 16, 16)], predp_r.at[k - 1], predp_ss, predp_rs, h_peer(k))

    backward(2, first=True)
    head_spread(3)
    backward(3)
    second_a(0)
    backward(1)
    second_a(1)
    second_c(0)
    backward(0, last=True)

    for k in range(1, 8):
        send(encp.at[(z + k) % 8], encp_r.at[k - 1], encp_ss, encp_rs, z_peer(k))
    second_a(2)
    second_c(1)
    second_b()
    drain(predp_r, predp_rs)
    predb[...] = predp[0:16, :] + predp_r[0] + predp_r[1] + predp_r[2]
    for k in range(1, 8):
        send(predb, predb_r.at[k - 1], predb_ss, predb_rs, f_peer(k))

    second_c(2)
    second_a(3, away=False)
    second_c(3, away=False)

    drain(p2a, p2_rs.at[0])
    a2 = a1[y] + p2a[0] + p2a[1] + p2a[2]
    drain(p2b, p2_rs.at[1])
    b2 = b1[own] + p2b[0] + p2b[1] + p2b[2]
    for zz in range(8):
        for n in range(2):
            ab2[zz, n, 0] = a2[zz, n * 4:n * 4 + 4, :]
            ab2[zz, n, 1] = b2[zz, n * 4:n * 4 + 4, :]
    for k in range(8):
        send(ab2.at[(z + k) % 8, 1 - core], p3oth.at[k], p3_ss.at[1], p3_rs.at[1], z_other(k))
        if k:
            send(ab2.at[(z + k) % 8, core], p3own.at[k - 1], p3_ss.at[0], p3_rs.at[0], z_peer(k))

    @pl.when(core == 0)
    def _():
        drain(p2c, p2_rs.at[2])
        tot = c1[y] + p2c[0] + p2c[1] + p2c[2]
        for n in range(2):
            c2[:, n] = tot[:, n * 4:n * 4 + 4, :]
        for k in range(4):
            send(c2.at[(x + k) % 4, 1], p3d.at[k], p3_ss.at[3], p3_rs.at[3], x_other(k))
            if k:
                send(c2.at[(x + k) % 4, 0], p3c.at[k - 1], p3_ss.at[2], p3_rs.at[2], x_peer(k))

    drain(encp_r, encp_rs)
    tot = encp[z]
    for k in range(7):
        tot = tot + encp_r[k]
    enc_out[...] = tot

    drain(predb_r, predb_rs)
    tot = predb[...]
    for k in range(7):
        tot = tot + predb_r[k]
    pred_out[...] = tot

    drain(p3own, p3_rs.at[0])
    tot = ab2[z, core]
    for k in range(7):
        tot = tot + p3own[k]
    fin[core, 0:2] = tot
    drain(p3oth, p3_rs.at[1])
    tot = p3oth[0]
    for k in range(1, 8):
        tot = tot + p3oth[k]
    fin[1 - core, 0:2] = tot

    @pl.when(core == 0)
    def _():
        drain(p3c, p3_rs.at[2])
        fin[0, 2] = c2[x, 0] + p3c[0] + p3c[1] + p3c[2]

    @pl.when(core == 1)
    def _():
        drain(p3d, p3_rs.at[3])
        fin[0, 2] = p3d[0] + p3d[1] + p3d[2] + p3d[3]

    for n in range(5):
        head_out[:, n * 128:n * 128 + 128] = fin[n // 3, n % 3]

    drain(msg_r, msg_ss)
    drain(part_r, part_ss)
    drain(encp_r, encp_ss)
    drain(predp_r, predp_ss)
    drain(predb_r, predb_ss)
    drain(h1ab, h1ab_ss)
    drain(p1a, p1_ss.at[0])
    drain(p1b, p1_ss.at[1])
    drain(p2a, p2_ss.at[0])
    drain(p2b, p2_ss.at[1])
    drain(p3own, p3_ss.at[0])
    drain(p3oth, p3_ss.at[1])

    @pl.when(core == 0)
    def _():
        drain(p1c, p1_ss.at[2])
        drain(p2c, p2_ss.at[2])
        drain(p3c, p3_ss.at[2])
        drain(p3d, p3_ss.at[3])

    @pl.when(core == 1)
    def _():
        drain(h1c, h1c_ss)


def hand_on(enc_in, pred_in, head_in, enc_out, pred_out, head_out):
    enc_out[...] = enc_in[...]
    pred_out[...] = pred_in[...]
    head_out[...] = head_in[...] * SCALE


def on_device(features, up_weight, down_weight, predictor, out_weight, blank_weight, label_weight, targets):
    V = pltpu.VMEM
    dma = pltpu.SemaphoreType.DMA
    scratch = [
        V((128, 1024), BF16), V((1024, 1024), BF16), V((1024, JD), BF16), V((JD, VOCAB), BF16),
        V((16, JD), BF16), V((16, 128), F32), V((16, 128), F32), dma((7,)),
        V((4, 16, JD + 128), F32), V((3, 16, JD + 128), F32), dma, dma((3,)),
        V((CH, 4, 8, JD), F32), V((CH, 3, 8, JD), F32), dma, dma((CH,)),
        V((LB, JD), F32), V((2048, 128), F32), V((2048, 128), F32), V((2048, 128), F32), V((LB, VOCAB), F32),
        V((FR, 8, JD), F32),
        V((2048, JD), BF16), V((2, CELLS, VOCAB), F32), V((2048, VOCAB), BF16), V((CELLS, JD), F32),
        V((8, 4, JD), F32), V((7, 4, JD), F32), dma, dma,
        V((LB, JD), F32), V((3, 16, JD), F32), dma, dma,
        V((16, JD), F32), V((7, 16, JD), F32), dma, dma,
        V((2, 4, 2, 32, 8, 128), F32), V((4, 32, 8, 128), F32),
        V((4, 2, 32, 8, 128), F32), V((4, 32, 8, 128), F32), dma, dma((4,)), dma, dma((4,)),
        V((4, 3, 8, 8, 128), F32), V((3, 32, 8, 128), F32), V((4, 7, 4, 8, 128), F32),
        dma((3,)), dma((4,)), dma, dma((4,)),
        V((4, 8, 8, 128), F32), V((32, 8, 128), F32), V((4, 4, 8, 128), F32),
        V((3, 8, 8, 128), F32), V((3, 8, 8, 128), F32), V((3, 4, 8, 128), F32), dma((3,)), dma((3,)),
        V((8, 2, 2, 4, 128), F32), V((4, 2, 4, 128), F32), V((7, 2, 4, 128), F32), V((8, 2, 4, 128), F32),
        V((3, 4, 128), F32), V((4, 4, 128), F32), dma((4,)), dma((4,)),
        V((2, 3, 4, 128), F32),
    ]
    hbm = pl.BlockSpec(memory_space=pl.ANY)
    vmem = pl.BlockSpec(memory_space=pltpu.VMEM)
    smem = pl.BlockSpec(memory_space=pltpu.SMEM)
    shapes = (
        jax.ShapeDtypeStruct((4, JD), F32),
        jax.ShapeDtypeStruct((16, JD), F32),
        jax.ShapeDtypeStruct((4, JD), F32),
    )
    results = pl.pallas_call(
        kernel,
        out_shape=shapes,
        in_specs=[hbm] * 7 + [smem],
        out_specs=(vmem, vmem, vmem),
        scratch_shapes=scratch,
        compiler_params=pltpu.CompilerParams(
            collective_id=0, has_side_effects=True, vmem_limit_bytes=60 * 1024 * 1024
        ),
    )(features, up_weight, down_weight, predictor, out_weight, blank_weight.T, label_weight.T, targets)
    return pl.pallas_call(
        hand_on, out_shape=shapes, in_specs=[vmem] * 3, out_specs=(vmem,) * 3
    )(*results)


def solution(mesh):
    placed = (
        P("frames", None),
        P(None, "hidden"),
        P("hidden", None),
        P(("labels", "hidden"), None),
        P(),
        P("frames", ("labels", "hidden")),
        P("frames", ("labels", "hidden")),
        P(("labels", "hidden")),
    )
    return jax.shard_map(
        on_device,
        mesh=mesh,
        in_specs=placed,
        out_specs=(
            P(("frames", "labels", "hidden"), None),
            P(("labels", "hidden"), None),
            P(("frames", "labels", "hidden"), None),
        ),
        check_vma=False,
    )
```

```python
import math

import jax
import jax.numpy as jnp
from jax import lax
from jax.experimental import pallas as pl
from jax.experimental.pallas import tpu as pltpu
from jax.sharding import PartitionSpec as P

F32 = jnp.float32
BF16 = jnp.bfloat16
JD = 640
VOCAB = 1024
FR = 32
LB = 64
CH = 4
FT = FR // CH
CELLS = FT * LB
RB = 16
SCALE = 1.0 / math.sqrt(1024 * 512)


def send(src, dst, send_sem, recv_sem, device):
    pltpu.make_async_remote_copy(
        src_ref=src,
        dst_ref=dst,
        send_sem=send_sem,
        recv_sem=recv_sem,
        device_id=device,
        device_id_type=pl.DeviceIdType.MESH,
    ).start()


def drain(ref, sem):
    pltpu.make_async_copy(ref, ref, sem).wait()


def kernel(
    feat_hbm, up_hbm, down_hbm, pred_hbm, w_hbm, blank_hbm, label_hbm, targets,
    enc_out, pred_out, head_out,
    feat, up, down, w, pred_in, blank_in, label_in, load_sem,
    msg, msg_r, msg_ss, msg_rs,
    tails, tails_r, tails_ss, tails_rs,
    part, part_r, part_ss, part_rs,
    pred64, wsum, wblank, wlabel, hot, encacc,
    joint, lg, grad, jg,
    encp, encp_r, encp_ss, encp_rs,
    predp, predp_r, predp_ss, predp_rs,
    predb, predb_r, predb_ss, predb_rs,
    predx_r, predy, predx_ss, predx_rs,
    hab, hc, h1ab, h1c, h1ab_ss, h1ab_rs, h1c_ss, h1c_rs,
    p1a, p1b, p1c, p1_ss, p1a_rs, p1b_rs, p1c_rs,
    a1, b1, c1, p2a, p2b, p2c, p2_ss, p2_rs,
    ab2, c2, p3own, p3oth, p3c, p3d, p3_ss, p3_rs,
    fin,
):
    f = lax.axis_index("frames")
    z = lax.axis_index("labels")
    h = lax.axis_index("hidden")
    y, x_lo = f // 2, f % 2
    x_hi, core = h // 2, h % 2
    x = x_hi * 2 + x_lo

    def h_of(s):
        return ((x_hi + s // 2) % 2) * 2 + (core + s % 2) % 2

    def h_peer(s):
        return {"hidden": h_of(s)}

    def z_peer(k):
        return {"labels": (z + k) % 8}

    def y_peer(k):
        return {"frames": ((y + k) % 4) * 2 + x_lo}

    def x_peer(k):
        xx = (x + k) % 4
        return {"frames": y * 2 + xx % 2, "hidden": (xx // 2) * 2 + core}

    def f_peer(k):
        return {"frames": (f + k) % 8}

    other = x_hi * 2 + (1 - core)
    partner = {"hidden": other}

    def z_other(k):
        return {"labels": (z + k) % 8, "hidden": other}

    def x_other(k):
        xx = (x + k) % 4
        return {"frames": y * 2 + xx % 2, "hidden": (xx // 2) * 2 + (1 - core)}

    barrier = pltpu.get_barrier_semaphore()
    greeted = [h_peer(s) for s in (1, 2, 3)] + [z_peer(k) for k in range(1, 8)]
    greeted += [f_peer(k) for k in range(1, 8)] + [x_peer(k) for k in (1, 3)]
    greeted += [z_other(k) for k in range(1, 8)] + [x_other(k) for k in (1, 3)]
    for device in greeted:
        pl.semaphore_signal(barrier, inc=1, device_id=device, device_id_type=pl.DeviceIdType.MESH)

    pairs = (
        (feat_hbm, feat), (blank_hbm, blank_in), (label_hbm, label_in), (pred_hbm, pred_in),
        (up_hbm, up), (down_hbm, down), (w_hbm, w),
    )
    loads = [pltpu.make_async_copy(a, b, load_sem.at[n]) for n, (a, b) in enumerate(pairs)]
    for load in loads:
        load.start()

    prow = lax.broadcasted_iota(jnp.int32, (128, 128), 0)
    pcol = lax.broadcasted_iota(jnp.int32, (128, 128), 1)
    pslot = (prow // 8) % 4
    pj = (prow // 32) * 8 + prow % 8
    pframe = (pj // 4) * 16 + h_of(pslot) * 4 + pj % 4
    perm = (pcol == pframe).astype(F32).astype(BF16)
    tcol = jnp.zeros((16, 128), jnp.int32)
    trow = lax.broadcasted_iota(jnp.int32, (16, 128), 0)
    for i in range(16):
        tcol = jnp.where(trow == i, targets[i], tcol)
    tfloat = tcol.astype(F32)
    lane = lax.broadcasted_iota(jnp.int32, (16, 128), 1) % 16
    for n in range(4):
        loads[n].wait()
    feat_p = jnp.dot(perm, feat[...], preferred_element_type=F32).astype(BF16)

    msg[...] = pred_in[...].astype(F32)
    for d in range(4):
        b = pltpu.roll(blank_in[...], (128 - 4 * d) % 128, 1)
        l = pltpu.roll(label_in[...], (132 - 4 * d) % 128, 1)
        tails[d] = jnp.where(lane < 4, b, jnp.where(lane < 8, l, tfloat))

    loads[4].wait()
    hidden = jnp.maximum(jnp.dot(feat_p, up[...], preferred_element_type=F32), 0.0).astype(BF16)

    pl.semaphore_wait(barrier, len(greeted))
    for s in (2, 1):
        send(msg, msg_r.at[s - 1], msg_ss, msg_rs.at[s - 1], h_peer(s))

    loads[5].wait()
    enc = jnp.dot(hidden, down[...], preferred_element_type=F32)
    for c in range(CH):
        for s in range(4):
            r = c * 32 + s * 8
            part[c, s] = enc[r:r + 8, :]
    for c in range(CH):
        for s in (2, 3, 1):
            send(part.at[c, s], part_r.at[c, s - 1], part_ss, part_rs.at[c], h_peer(s))
        if c == 0:
            for s in (2, 3, 1):
                send(tails.at[h_of(s)], tails_r.at[s - 1], tails_ss, tails_rs.at[s - 1], h_peer(s))

    vocab_id = lax.broadcasted_iota(jnp.int32, (RB, 128), 1).astype(F32)

    def labels_of(k):
        if k:
            drain(tails_r.at[k - 1], tails_rs.at[k - 1])
            if k != 2:
                drain(msg_r.at[k - 1], msg_rs.at[k - 1])
        src = msg_r.at[k - 1] if k else msg
        rows = slice(k * 16, k * 16 + 16)
        pred64[rows, :] = src[...]
        tail = tails_r[k - 1] if k else tails[h]
        tg = jnp.broadcast_to(tail[:, 8:9], (16, 128))
        for n in range(8):
            hot[rows, n * 128:n * 128 + 128] = jnp.where(vocab_id == tg - float(n * 128), 1.0, 0.0)
        for t in range(FR):
            r = (k * FR + t) * 16
            at = (t // 4) * 16 + t % 4
            b = jnp.broadcast_to(tail[:, at:at + 1], (16, 128))
            l = jnp.broadcast_to(tail[:, at + 4:at + 5], (16, 128))
            wsum[r:r + 16, :] = b + l
            wblank[r:r + 16, :] = b
            wlabel[r:r + 16, :] = l

    labels_of(0)
    drain(msg_r.at[1], msg_rs.at[1])
    send(msg_r.at[1], msg_r.at[2], msg_ss, msg_rs.at[2], h_peer(1))
    for k in (1, 2, 3):
        labels_of(k)
    loads[6].wait()

    def logits_of(c):
        drain(part_r.at[c], part_rs.at[c])
        enc8 = part[c, 0] + part_r[c, 0] + part_r[c, 1] + part_r[c, 2]
        for t in range(FT):
            cells = jnp.tanh(pred64[...] + enc8[t:t + 1, :]).astype(BF16)
            for k in range(4):
                r = (k * FR + c * FT + t) * 16
                joint[r:r + 16, :] = cells[k * 16:k * 16 + 16, :]
        ends = [(k * FR + c * FT) * 16 for k in range(4)]
        lhs = jnp.concatenate([joint[r:r + FT * 16, :] for r in ends], axis=0)
        lg[c % 2] = jnp.dot(lhs, w[...], preferred_element_type=F32)

    def softmax_of(c):
        for i in range(CELLS // RB):
            rows = slice(i * RB, i * RB + RB)
            block, t = i // FT, c * FT + i % FT
            r = (block * FR + t) * 16
            cell = slice(r, r + 16)
            label = slice(block * 16, block * 16 + 16)
            tiles = [lg[c % 2, rows, n * 128:n * 128 + 128] for n in range(8)]
            m = tiles[0]
            for tile in tiles[1:]:
                m = jnp.maximum(m, tile)
            top = jnp.max(m, axis=1, keepdims=True)
            exps = [jnp.exp(tile - top) for tile in tiles]
            s = exps[0]
            for e in exps[1:]:
                s = s + e
            scale = wsum[cell, :] / jnp.sum(s, axis=1, keepdims=True)
            lw = wlabel[cell, :]
            for n in range(8):
                g = exps[n] * scale - lw * hot[label, n * 128:n * 128 + 128]
                if n == 0:
                    g = g - jnp.where(vocab_id == 0.0, wblank[cell, :], 0.0)
                grad[cell, n * 128:n * 128 + 128] = g.astype(BF16)

    logits_of(0)
    for c in range(1, 4):
        logits_of(c)
        softmax_of(c - 1)
    softmax_of(3)

    def head_block(i):
        yy = (y + 1 + i) % 4
        col = pl.multiple_of(yy * 256, 256)
        block = lax.dot_general(
            grad[:, pl.ds(col, 256)], joint[...], (((0,), (0,)), ((), ())),
            preferred_element_type=F32,
        )
        for t in range(32):
            xl, zz, xh = t // 16, (t // 2) % 8, t % 2
            xx = xh * 2 + xl
            rows = block[t * 8:t * 8 + 8, :]
            hab[0, yy, 0, xx * 8 + zz] = rows[:, 0:128]
            hab[0, yy, 1, xx * 8 + zz] = rows[:, 128:256]
            hc[yy, zz * 4 + xx] = rows[:, 256:384]
            hab[1, yy, 0, xx * 8 + zz] = rows[:, 384:512]
            hab[1, yy, 1, xx * 8 + zz] = rows[:, 512:640]
        send(hab.at[1 - core, yy], h1ab.at[yy], h1ab_ss, h1ab_rs.at[yy], partner)

        @pl.when(core == 1)
        def _():
            send(hc.at[yy], h1c.at[yy], h1c_ss, h1c_rs.at[yy], partner)

    def head_spread(i):
        yy = (y + 1 + i) % 4
        drain(h1ab.at[yy], h1ab_rs.at[yy])
        hab[core, yy] = hab[core, yy] + h1ab[yy]
        for k in (1, 2, 3):
            at = pl.multiple_of(((x + k) % 4) * 8, 8)
            send(hab.at[core, yy, 0, pl.ds(at, 8)], p1a.at[yy, k - 1], p1_ss.at[0], p1a_rs.at[yy], x_peer(k))

        @pl.when(i < 3)
        def _():
            send(hab.at[core, yy, 1], p1b.at[i], p1_ss.at[1], p1b_rs, {"frames": yy * 2 + x_lo})

        @pl.when(core == 0)
        def _():
            drain(h1c.at[yy], h1c_rs.at[yy])
            hc[yy] = hc[yy] + h1c[yy]
            for k in range(1, 8):
                at = pl.multiple_of(((z + k) % 8) * 4, 4)
                send(hc.at[yy, pl.ds(at, 4)], p1c.at[yy, k - 1], p1_ss.at[2], p1c_rs.at[yy], z_peer(k))

    own = pl.ds(pl.multiple_of(x * 8, 8), 8)
    mine = pl.ds(pl.multiple_of(z * 4, 4), 4)

    def second_a(i, away=True):
        yy = (y + 1 + i) % 4
        drain(p1a.at[yy], p1a_rs.at[yy])
        a1[yy] = hab[core, yy, 0, own] + p1a[yy, 0] + p1a[yy, 1] + p1a[yy, 2]
        if away:
            send(a1.at[yy], p2a.at[i], p2_ss.at[0], p2_rs.at[0], {"frames": yy * 2 + x_lo})

    def second_b():
        drain(p1b, p1b_rs)
        b1[...] = hab[core, y, 1] + p1b[0] + p1b[1] + p1b[2]
        for k in (1, 2, 3):
            at = pl.multiple_of(((x + k) % 4) * 8, 8)
            send(b1.at[pl.ds(at, 8)], p2b.at[k - 1], p2_ss.at[1], p2_rs.at[1], x_peer(k))

    def second_c(i, away=True):
        @pl.when(core == 0)
        def _():
            yy = (y + 1 + i) % 4
            drain(p1c.at[yy], p1c_rs.at[yy])
            tot = hc[yy, mine]
            for k in range(7):
                tot = tot + p1c[yy, k]
            c1[yy] = tot
            if away:
                send(c1.at[yy], p2c.at[i], p2_ss.at[2], p2_rs.at[2], {"frames": yy * 2 + x_lo})

    def head_step(i, carry):
        head_block(i)

        @pl.when(i > 0)
        def _():
            head_spread(i - 1)

        return carry

    lax.fori_loop(0, 4, head_step, 0)

    def backward(k, first=False, last=False):
        r = k * FR * 16
        jg[...] = lax.dot_general(
            grad[r:r + FR * 16, :], w[...], (((1,), (1,)), ((), ())), preferred_element_type=F32
        )
        for n in range(5):
            cols = slice(n * 128, n * 128 + 128)
            acc = jnp.zeros((16, 128), F32)
            for t in range(FR):
                cells = joint[r + t * 16:r + t * 16 + 16, cols].astype(F32)
                tg = jg[t * 16:t * 16 + 16, cols] * (1.0 - cells * cells)
                acc = acc + tg
                both = tg[0:8, :] + tg[8:16, :]
                if not first:
                    both = both + encacc[t, :, cols]
                if last:
                    encp[t // 4, t % 4:t % 4 + 1, cols] = jnp.sum(both, axis=0, keepdims=True)
                else:
                    encacc[t, :, cols] = both
            predp[k * 16:k * 16 + 16, cols] = acc
        if k:
            send(predp.at[pl.ds(k * 16, 16)], predp_r.at[k - 1], predp_ss, predp_rs, h_peer(k))

    backward(2, first=True)
    head_spread(3)
    backward(3)
    second_a(0)
    backward(1)
    second_a(1)
    second_c(0)
    backward(0, last=True)

    for k in range(1, 8):
        send(encp.at[(z + k) % 8], encp_r.at[k - 1], encp_ss, encp_rs, z_peer(k))
    second_a(2)
    second_c(1)
    second_b()
    drain(predp_r, predp_rs)
    predb[...] = predp[0:16, :] + predp_r[0] + predp_r[1] + predp_r[2]
    send(predb, predx_r, predx_ss, predx_rs, {"frames": y * 2 + 1 - x_lo})

    second_c(2)
    second_a(3, away=False)
    second_c(3, away=False)

    drain(predx_r, predx_rs)
    predy[...] = predb[...] + predx_r[...]
    for k in (1, 2, 3):
        send(predy, predb_r.at[k - 1], predb_ss, predb_rs, y_peer(k))

    drain(p2a, p2_rs.at[0])
    a2 = a1[y] + p2a[0] + p2a[1] + p2a[2]
    drain(p2b, p2_rs.at[1])
    b2 = b1[own] + p2b[0] + p2b[1] + p2b[2]
    for zz in range(8):
        for n in range(2):
            ab2[zz, n, 0] = a2[zz, n * 4:n * 4 + 4, :]
            ab2[zz, n, 1] = b2[zz, n * 4:n * 4 + 4, :]
    for k in range(8):
        send(ab2.at[(z + k) % 8, 1 - core], p3oth.at[k], p3_ss.at[1], p3_rs.at[1], z_other(k))
        if k:
            send(ab2.at[(z + k) % 8, core], p3own.at[k - 1], p3_ss.at[0], p3_rs.at[0], z_peer(k))

    @pl.when(core == 0)
    def _():
        drain(p2c, p2_rs.at[2])
        tot = c1[y] + p2c[0] + p2c[1] + p2c[2]
        for n in range(2):
            c2[:, n] = tot[:, n * 4:n * 4 + 4, :]
        for k in range(4):
            send(c2.at[(x + k) % 4, 1], p3d.at[k], p3_ss.at[3], p3_rs.at[3], x_other(k))
            if k:
                send(c2.at[(x + k) % 4, 0], p3c.at[k - 1], p3_ss.at[2], p3_rs.at[2], x_peer(k))

    drain(encp_r, encp_rs)
    tot = encp[z]
    for k in range(7):
        tot = tot + encp_r[k]
    enc_out[...] = tot

    drain(predb_r, predb_rs)
    pred_out[...] = predy[...] + predb_r[0] + predb_r[1] + predb_r[2]

    drain(p3own, p3_rs.at[0])
    tot = ab2[z, core]
    for k in range(7):
        tot = tot + p3own[k]
    fin[core, 0:2] = tot
    drain(p3oth, p3_rs.at[1])
    tot = p3oth[0]
    for k in range(1, 8):
        tot = tot + p3oth[k]
    fin[1 - core, 0:2] = tot

    @pl.when(core == 0)
    def _():
        drain(p3c, p3_rs.at[2])
        fin[0, 2] = c2[x, 0] + p3c[0] + p3c[1] + p3c[2]

    @pl.when(core == 1)
    def _():
        drain(p3d, p3_rs.at[3])
        fin[0, 2] = p3d[0] + p3d[1] + p3d[2] + p3d[3]

    for n in range(5):
        head_out[:, n * 128:n * 128 + 128] = fin[n // 3, n % 3]

    drain(msg_r, msg_ss)
    drain(tails_r, tails_ss)
    drain(part_r, part_ss)
    drain(encp_r, encp_ss)
    drain(predp_r, predp_ss)
    drain(predb_r, predb_ss)
    drain(predx_r, predx_ss)
    drain(h1ab, h1ab_ss)
    drain(p1a, p1_ss.at[0])
    drain(p1b, p1_ss.at[1])
    drain(p2a, p2_ss.at[0])
    drain(p2b, p2_ss.at[1])
    drain(p3own, p3_ss.at[0])
    drain(p3oth, p3_ss.at[1])

    @pl.when(core == 0)
    def _():
        drain(p1c, p1_ss.at[2])
        drain(p2c, p2_ss.at[2])
        drain(p3c, p3_ss.at[2])
        drain(p3d, p3_ss.at[3])

    @pl.when(core == 1)
    def _():
        drain(h1c, h1c_ss)


def hand_on(enc_in, pred_in, head_in, enc_out, pred_out, head_out):
    enc_out[...] = enc_in[...]
    pred_out[...] = pred_in[...]
    head_out[...] = head_in[...] * SCALE


def on_device(features, up_weight, down_weight, predictor, out_weight, blank_weight, label_weight, targets):
    V = pltpu.VMEM
    dma = pltpu.SemaphoreType.DMA
    scratch = [
        V((128, 1024), BF16), V((1024, 1024), BF16), V((1024, JD), BF16), V((JD, VOCAB), BF16),
        V((16, JD), BF16), V((16, 128), F32), V((16, 128), F32), dma((7,)),
        V((16, JD), F32), V((3, 16, JD), F32), dma, dma((3,)),
        V((4, 16, 128), F32), V((3, 16, 128), F32), dma, dma((3,)),
        V((CH, 4, 8, JD), F32), V((CH, 3, 8, JD), F32), dma, dma((CH,)),
        V((LB, JD), F32), V((2048, 128), F32), V((2048, 128), F32), V((2048, 128), F32), V((LB, VOCAB), F32),
        V((FR, 8, JD), F32),
        V((2048, JD), BF16), V((2, CELLS, VOCAB), F32), V((2048, VOCAB), BF16), V((CELLS, JD), F32),
        V((8, 4, JD), F32), V((7, 4, JD), F32), dma, dma,
        V((LB, JD), F32), V((3, 16, JD), F32), dma, dma,
        V((16, JD), F32), V((3, 16, JD), F32), dma, dma,
        V((16, JD), F32), V((16, JD), F32), dma, dma,
        V((2, 4, 2, 32, 8, 128), F32), V((4, 32, 8, 128), F32),
        V((4, 2, 32, 8, 128), F32), V((4, 32, 8, 128), F32), dma, dma((4,)), dma, dma((4,)),
        V((4, 3, 8, 8, 128), F32), V((3, 32, 8, 128), F32), V((4, 7, 4, 8, 128), F32),
        dma((3,)), dma((4,)), dma, dma((4,)),
        V((4, 8, 8, 128), F32), V((32, 8, 128), F32), V((4, 4, 8, 128), F32),
        V((3, 8, 8, 128), F32), V((3, 8, 8, 128), F32), V((3, 4, 8, 128), F32), dma((3,)), dma((3,)),
        V((8, 2, 2, 4, 128), F32), V((4, 2, 4, 128), F32), V((7, 2, 4, 128), F32), V((8, 2, 4, 128), F32),
        V((3, 4, 128), F32), V((4, 4, 128), F32), dma((4,)), dma((4,)),
        V((2, 3, 4, 128), F32),
    ]
    hbm = pl.BlockSpec(memory_space=pl.ANY)
    vmem = pl.BlockSpec(memory_space=pltpu.VMEM)
    smem = pl.BlockSpec(memory_space=pltpu.SMEM)
    shapes = (
        jax.ShapeDtypeStruct((4, JD), F32),
        jax.ShapeDtypeStruct((16, JD), F32),
        jax.ShapeDtypeStruct((4, JD), F32),
    )
    results = pl.pallas_call(
        kernel,
        out_shape=shapes,
        in_specs=[hbm] * 7 + [smem],
        out_specs=(vmem, vmem, vmem),
        scratch_shapes=scratch,
        compiler_params=pltpu.CompilerParams(
            collective_id=0, has_side_effects=True, vmem_limit_bytes=60 * 1024 * 1024
        ),
    )(features, up_weight, down_weight, predictor, out_weight, blank_weight.T, label_weight.T, targets)
    return pl.pallas_call(
        hand_on, out_shape=shapes, in_specs=[vmem] * 3, out_specs=(vmem,) * 3
    )(*results)


def solution(mesh):
    placed = (
        P("frames", None),
        P(None, "hidden"),
        P("hidden", None),
        P(("labels", "hidden"), None),
        P(),
        P("frames", ("labels", "hidden")),
        P("frames", ("labels", "hidden")),
        P(("labels", "hidden")),
    )
    return jax.shard_map(
        on_device,
        mesh=mesh,
        in_specs=placed,
        out_specs=(
            P(("frames", "labels", "hidden"), None),
            P(("labels", "hidden"), None),
            P(("frames", "labels", "hidden"), None),
        ),
        check_vma=False,
    )
```

```python
import math

import jax
import jax.numpy as jnp
from jax import lax
from jax.experimental import pallas as pl
from jax.experimental.pallas import tpu as pltpu
from jax.sharding import PartitionSpec as P

F32 = jnp.float32
BF16 = jnp.bfloat16
JD = 640
VOCAB = 1024
FR = 32
LB = 64
CH = 4
FT = FR // CH
CELLS = FT * LB
RB = 16
SCALE = 1.0 / math.sqrt(1024 * 512)


def send(src, dst, send_sem, recv_sem, device):
    pltpu.make_async_remote_copy(
        src_ref=src,
        dst_ref=dst,
        send_sem=send_sem,
        recv_sem=recv_sem,
        device_id=device,
        device_id_type=pl.DeviceIdType.MESH,
    ).start()


def drain(ref, sem):
    pltpu.make_async_copy(ref, ref, sem).wait()


def kernel(
    feat_hbm, up_hbm, down_hbm, pred_hbm, w_hbm, blank_hbm, label_hbm, targets,
    enc_out, pred_out, head_out,
    feat, up, down, w, pred_in, blank_in, label_in, load_sem,
    msg, msg_r, msg_ss, msg_rs,
    tails, tails_r, tails_ss, tails_rs,
    part, part_r, part_ss, part_rs,
    pred64, wsum, wblank, wlabel, hot, encacc,
    joint, lg, grad, jg,
    encp, encp_r, encp_ss, encp_rs,
    predp, predp_r, predp_ss, predp_rs,
    predb, predb_r, predb_ss, predb_rs,
    predx_r, predy, predx_ss, predx_rs,
    hab, hc, h1ab, h1c, h1ab_ss, h1ab_rs, h1c_ss, h1c_rs,
    p1a, p1b, p1c, p1_ss, p1a_rs, p1b_rs, p1c_rs,
    a1, b1, c1, p2a, p2b, p2c, p2_ss, p2_rs,
    ab2, c2, p3own, p3oth, p3c, p3d, p3_ss, p3_rs, p3o_rs,
    fin,
):
    f = lax.axis_index("frames")
    z = lax.axis_index("labels")
    h = lax.axis_index("hidden")
    y, x_lo = f // 2, f % 2
    x_hi, core = h // 2, h % 2
    x = x_hi * 2 + x_lo

    def h_of(s):
        return ((x_hi + s // 2) % 2) * 2 + (core + s % 2) % 2

    def h_peer(s):
        return {"hidden": h_of(s)}

    def z_peer(k):
        return {"labels": (z + k) % 8}

    def y_peer(k):
        return {"frames": ((y + k) % 4) * 2 + x_lo}

    def x_peer(k):
        xx = (x + k) % 4
        return {"frames": y * 2 + xx % 2, "hidden": (xx // 2) * 2 + core}

    other = x_hi * 2 + (1 - core)
    partner = {"hidden": other}

    def z_other(k):
        return {"labels": (z + k) % 8, "hidden": other}

    def x_other(k):
        xx = (x + k) % 4
        return {"frames": y * 2 + xx % 2, "hidden": (xx // 2) * 2 + (1 - core)}

    barrier = pltpu.get_barrier_semaphore()
    greeted = [h_peer(s) for s in (1, 2, 3)] + [z_peer(k) for k in range(1, 8)]
    greeted += [y_peer(k) for k in (1, 2, 3)] + [x_peer(k) for k in (1, 3)]
    greeted += [z_other(k) for k in range(1, 8)] + [x_other(k) for k in (1, 3)]
    for device in greeted:
        pl.semaphore_signal(barrier, inc=1, device_id=device, device_id_type=pl.DeviceIdType.MESH)

    pairs = (
        (feat_hbm, feat), (blank_hbm, blank_in), (label_hbm, label_in), (pred_hbm, pred_in),
        (up_hbm, up), (down_hbm, down), (w_hbm, w),
    )
    loads = [pltpu.make_async_copy(a, b, load_sem.at[n]) for n, (a, b) in enumerate(pairs)]
    for load in loads:
        load.start()

    prow = lax.broadcasted_iota(jnp.int32, (128, 128), 0)
    pcol = lax.broadcasted_iota(jnp.int32, (128, 128), 1)
    pslot = (prow // 8) % 4
    pj = (prow // 32) * 8 + prow % 8
    pframe = (pj // 4) * 16 + h_of(pslot) * 4 + pj % 4
    perm = (pcol == pframe).astype(F32).astype(BF16)
    for n in range(4):
        loads[n].wait()
    feat_p = jnp.dot(perm, feat[...], preferred_element_type=F32).astype(BF16)

    msg[...] = pred_in[...].astype(F32)
    loads[4].wait()
    hidden = jnp.maximum(jnp.dot(feat_p, up[...], preferred_element_type=F32), 0.0).astype(BF16)

    def build_tails():
        tcol = jnp.zeros((16, 128), jnp.int32)
        trow = lax.broadcasted_iota(jnp.int32, (16, 128), 0)
        for i in range(16):
            tcol = jnp.where(trow == i, targets[i], tcol)
        tfloat = tcol.astype(F32)
        lane = lax.broadcasted_iota(jnp.int32, (16, 128), 1) % 16

        for d in range(4):
            b = pltpu.roll(blank_in[...], (128 - 4 * d) % 128, 1)
            l = pltpu.roll(label_in[...], (132 - 4 * d) % 128, 1)
            tails[d] = jnp.where(lane < 4, b, jnp.where(lane < 8, l, tfloat))

    pl.semaphore_wait(barrier, len(greeted))
    for s in (2, 1):
        send(msg, msg_r.at[s - 1], msg_ss, msg_rs.at[s - 1], h_peer(s))

    loads[5].wait()
    enc = jnp.dot(hidden, down[...], preferred_element_type=F32)
    for c in range(CH):
        for s in range(4):
            r = c * 32 + s * 8
            part[c, s] = enc[r:r + 8, :]
    for c in range(CH):
        for s in (2, 3, 1):
            send(part.at[c, s], part_r.at[c, s - 1], part_ss, part_rs.at[c], h_peer(s))
        if c == 0:
            build_tails()
            for s in (2, 3, 1):
                send(tails.at[h_of(s)], tails_r.at[s - 1], tails_ss, tails_rs.at[s - 1], h_peer(s))

    vocab_id = lax.broadcasted_iota(jnp.int32, (RB, 128), 1).astype(F32)

    def labels_of(k):
        if k:
            drain(tails_r.at[k - 1], tails_rs.at[k - 1])
            if k != 2:
                drain(msg_r.at[k - 1], msg_rs.at[k - 1])
        src = msg_r.at[k - 1] if k else msg
        rows = slice(k * 16, k * 16 + 16)
        pred64[rows, :] = src[...]
        tail = tails_r[k - 1] if k else tails[h]
        tg = jnp.broadcast_to(tail[:, 8:9], (16, 128))
        for n in range(8):
            hot[rows, n * 128:n * 128 + 128] = jnp.where(vocab_id == tg - float(n * 128), 1.0, 0.0)
        for t in range(FR):
            r = (k * FR + t) * 16
            at = (t // 4) * 16 + t % 4
            b = jnp.broadcast_to(tail[:, at:at + 1], (16, 128))
            l = jnp.broadcast_to(tail[:, at + 4:at + 5], (16, 128))
            wsum[r:r + 16, :] = b + l
            wblank[r:r + 16, :] = b
            wlabel[r:r + 16, :] = l

    labels_of(0)
    drain(msg_r.at[1], msg_rs.at[1])
    send(msg_r.at[1], msg_r.at[2], msg_ss, msg_rs.at[2], h_peer(1))
    for k in (1, 2, 3):
        labels_of(k)
    loads[6].wait()

    def logits_of(c):
        drain(part_r.at[c], part_rs.at[c])
        enc8 = part[c, 0] + part_r[c, 0] + part_r[c, 1] + part_r[c, 2]
        for t in range(FT):
            cells = jnp.tanh(pred64[...] + enc8[t:t + 1, :]).astype(BF16)
            for k in range(4):
                r = (k * FR + c * FT + t) * 16
                joint[r:r + 16, :] = cells[k * 16:k * 16 + 16, :]
        ends = [(k * FR + c * FT) * 16 for k in range(4)]
        lhs = jnp.concatenate([joint[r:r + FT * 16, :] for r in ends], axis=0)
        lg[c % 2] = jnp.dot(lhs, w[...], preferred_element_type=F32)

    def softmax_of(c):
        for i in range(CELLS // RB):
            rows = slice(i * RB, i * RB + RB)
            block, t = i // FT, c * FT + i % FT
            r = (block * FR + t) * 16
            cell = slice(r, r + 16)
            label = slice(block * 16, block * 16 + 16)
            tiles = [lg[c % 2, rows, n * 128:n * 128 + 128] for n in range(8)]
            m = tiles[0]
            for tile in tiles[1:]:
                m = jnp.maximum(m, tile)
            top = jnp.max(m, axis=1, keepdims=True)
            exps = [jnp.exp(tile - top) for tile in tiles]
            s = exps[0]
            for e in exps[1:]:
                s = s + e
            scale = wsum[cell, :] / jnp.sum(s, axis=1, keepdims=True)
            lw = wlabel[cell, :]
            for n in range(8):
                g = exps[n] * scale - lw * hot[label, n * 128:n * 128 + 128]
                if n == 0:
                    g = g - jnp.where(vocab_id == 0.0, wblank[cell, :], 0.0)
                grad[cell, n * 128:n * 128 + 128] = g.astype(BF16)

    logits_of(0)
    for c in range(1, 4):
        logits_of(c)
        softmax_of(c - 1)
    softmax_of(3)

    def head_block(i):
        yy = (y + 1 + i) % 4
        col = pl.multiple_of(yy * 256, 256)
        block = lax.dot_general(
            grad[:, pl.ds(col, 256)], joint[...], (((0,), (0,)), ((), ())),
            preferred_element_type=F32,
        )
        for t in range(32):
            xl, zz, xh = t // 16, (t // 2) % 8, t % 2
            xx = xh * 2 + xl
            rows = block[t * 8:t * 8 + 8, :]
            hab[0, yy, 0, xx * 8 + zz] = rows[:, 0:128]
            hab[0, yy, 1, xx * 8 + zz] = rows[:, 128:256]
            hc[yy, zz * 4 + xx] = rows[:, 256:384]
            hab[1, yy, 0, xx * 8 + zz] = rows[:, 384:512]
            hab[1, yy, 1, xx * 8 + zz] = rows[:, 512:640]
        send(hab.at[1 - core, yy], h1ab.at[yy], h1ab_ss, h1ab_rs.at[yy], partner)

        @pl.when(core == 1)
        def _():
            send(hc.at[yy], h1c.at[yy], h1c_ss, h1c_rs.at[yy], partner)

    def head_spread(i):
        yy = (y + 1 + i) % 4
        drain(h1ab.at[yy], h1ab_rs.at[yy])
        hab[core, yy] = hab[core, yy] + h1ab[yy]
        for k in (1, 2, 3):
            at = pl.multiple_of(((x + k) % 4) * 8, 8)
            send(hab.at[core, yy, 0, pl.ds(at, 8)], p1a.at[yy, k - 1], p1_ss.at[0], p1a_rs.at[yy], x_peer(k))

        @pl.when(i < 3)
        def _():
            send(hab.at[core, yy, 1], p1b.at[i], p1_ss.at[1], p1b_rs, {"frames": yy * 2 + x_lo})

        @pl.when(core == 0)
        def _():
            drain(h1c.at[yy], h1c_rs.at[yy])
            hc[yy] = hc[yy] + h1c[yy]
            for k in range(1, 8):
                at = pl.multiple_of(((z + k) % 8) * 4, 4)
                send(hc.at[yy, pl.ds(at, 4)], p1c.at[yy, k - 1], p1_ss.at[2], p1c_rs.at[yy], z_peer(k))

    own = pl.ds(pl.multiple_of(x * 8, 8), 8)
    mine = pl.ds(pl.multiple_of(z * 4, 4), 4)

    def second_a(i, away=True):
        yy = (y + 1 + i) % 4
        drain(p1a.at[yy], p1a_rs.at[yy])
        a1[yy] = hab[core, yy, 0, own] + p1a[yy, 0] + p1a[yy, 1] + p1a[yy, 2]
        if away:
            send(a1.at[yy], p2a.at[i], p2_ss.at[0], p2_rs.at[0], {"frames": yy * 2 + x_lo})

    def second_b():
        drain(p1b, p1b_rs)
        b1[...] = hab[core, y, 1] + p1b[0] + p1b[1] + p1b[2]
        for k in (1, 2, 3):
            at = pl.multiple_of(((x + k) % 4) * 8, 8)
            send(b1.at[pl.ds(at, 8)], p2b.at[k - 1], p2_ss.at[1], p2_rs.at[1], x_peer(k))

    def second_c(i, away=True):
        @pl.when(core == 0)
        def _():
            yy = (y + 1 + i) % 4
            drain(p1c.at[yy], p1c_rs.at[yy])
            tot = hc[yy, mine]
            for k in range(7):
                tot = tot + p1c[yy, k]
            c1[yy] = tot
            if away:
                send(c1.at[yy], p2c.at[i], p2_ss.at[2], p2_rs.at[2], {"frames": yy * 2 + x_lo})

    def head_step(i, carry):
        head_block(i)

        @pl.when(i > 0)
        def _():
            head_spread(i - 1)

        return carry

    lax.fori_loop(0, 4, head_step, 0)

    def backward(k, first=False, last=False):
        r = k * FR * 16
        jg[...] = lax.dot_general(
            grad[r:r + FR * 16, :], w[...], (((1,), (1,)), ((), ())), preferred_element_type=F32
        )
        for n in range(5):
            cols = slice(n * 128, n * 128 + 128)
            acc = jnp.zeros((16, 128), F32)
            for t in range(FR):
                cells = joint[r + t * 16:r + t * 16 + 16, cols].astype(F32)
                tg = jg[t * 16:t * 16 + 16, cols] * (1.0 - cells * cells)
                acc = acc + tg
                both = tg[0:8, :] + tg[8:16, :]
                if not first:
                    both = both + encacc[t, :, cols]
                if last:
                    encp[t // 4, t % 4:t % 4 + 1, cols] = jnp.sum(both, axis=0, keepdims=True)
                else:
                    encacc[t, :, cols] = both
            predp[k * 16:k * 16 + 16, cols] = acc
        if k:
            send(predp.at[pl.ds(k * 16, 16)], predp_r.at[k - 1], predp_ss, predp_rs, h_peer(k))

    backward(2, first=True)
    head_spread(3)
    backward(3)
    second_a(0)
    backward(1)
    second_a(1)
    second_c(0)
    backward(0, last=True)

    for k in range(1, 8):
        send(encp.at[(z + k) % 8], encp_r.at[k - 1], encp_ss, encp_rs, z_peer(k))
    second_a(2)
    second_c(1)
    second_b()
    drain(predp_r, predp_rs)
    predb[...] = predp[0:16, :] + predp_r[0] + predp_r[1] + predp_r[2]
    send(predb, predx_r, predx_ss, predx_rs, {"frames": y * 2 + 1 - x_lo})

    second_c(2)
    second_a(3, away=False)
    second_c(3, away=False)

    drain(predx_r, predx_rs)
    predy[...] = predb[...] + predx_r[...]
    for k in (1, 2, 3):
        send(predy, predb_r.at[k - 1], predb_ss, predb_rs, y_peer(k))

    def third(n, tot):
        for zz in range(8):
            for half in range(2):
                ab2[n, zz, half] = tot[zz, half * 4:half * 4 + 4, :]
        for k in range(8):
            send(ab2.at[n, (z + k) % 8, 1 - core], p3oth.at[n, k], p3_ss.at[1], p3o_rs.at[n], z_other(k))
            if k:
                send(ab2.at[n, (z + k) % 8, core], p3own.at[n, k - 1], p3_ss.at[0], p3_rs.at[n], z_peer(k))

    drain(p2a, p2_rs.at[0])
    third(0, a1[y] + p2a[0] + p2a[1] + p2a[2])
    drain(p2b, p2_rs.at[1])
    third(1, b1[own] + p2b[0] + p2b[1] + p2b[2])
    @pl.when(core == 0)
    def _():
        drain(p2c, p2_rs.at[2])
        tot = c1[y] + p2c[0] + p2c[1] + p2c[2]
        for n in range(2):
            c2[:, n] = tot[:, n * 4:n * 4 + 4, :]
        for k in range(4):
            send(c2.at[(x + k) % 4, 1], p3d.at[k], p3_ss.at[3], p3_rs.at[3], x_other(k))
            if k:
                send(c2.at[(x + k) % 4, 0], p3c.at[k - 1], p3_ss.at[2], p3_rs.at[2], x_peer(k))

    drain(encp_r, encp_rs)
    tot = encp[z]
    for k in range(7):
        tot = tot + encp_r[k]
    enc_out[...] = tot

    drain(predb_r, predb_rs)
    pred_out[...] = predy[...] + predb_r[0] + predb_r[1] + predb_r[2]

    for n in range(2):
        drain(p3own.at[n], p3_rs.at[n])
        tot = ab2[n, z, core]
        for k in range(7):
            tot = tot + p3own[n, k]
        fin[core, n] = tot
        drain(p3oth.at[n], p3o_rs.at[n])
        tot = p3oth[n, 0]
        for k in range(1, 8):
            tot = tot + p3oth[n, k]
        fin[1 - core, n] = tot

    @pl.when(core == 0)
    def _():
        drain(p3c, p3_rs.at[2])
        fin[0, 2] = c2[x, 0] + p3c[0] + p3c[1] + p3c[2]

    @pl.when(core == 1)
    def _():
        drain(p3d, p3_rs.at[3])
        fin[0, 2] = p3d[0] + p3d[1] + p3d[2] + p3d[3]

    for n in range(5):
        head_out[:, n * 128:n * 128 + 128] = fin[n // 3, n % 3]

    drain(msg_r, msg_ss)
    drain(tails_r, tails_ss)
    drain(part_r, part_ss)
    drain(encp_r, encp_ss)
    drain(predp_r, predp_ss)
    drain(predb_r, predb_ss)
    drain(predx_r, predx_ss)
    drain(h1ab, h1ab_ss)
    drain(p1a, p1_ss.at[0])
    drain(p1b, p1_ss.at[1])
    drain(p2a, p2_ss.at[0])
    drain(p2b, p2_ss.at[1])
    drain(p3own, p3_ss.at[0])
    drain(p3oth, p3_ss.at[1])

    @pl.when(core == 0)
    def _():
        drain(p1c, p1_ss.at[2])
        drain(p2c, p2_ss.at[2])
        drain(p3c, p3_ss.at[2])
        drain(p3d, p3_ss.at[3])

    @pl.when(core == 1)
    def _():
        drain(h1c, h1c_ss)


def hand_on(enc_in, pred_in, head_in, enc_out, pred_out, head_out):
    enc_out[...] = enc_in[...]
    pred_out[...] = pred_in[...]
    head_out[...] = head_in[...] * SCALE


def on_device(features, up_weight, down_weight, predictor, out_weight, blank_weight, label_weight, targets):
    V = pltpu.VMEM
    dma = pltpu.SemaphoreType.DMA
    scratch = [
        V((128, 1024), BF16), V((1024, 1024), BF16), V((1024, JD), BF16), V((JD, VOCAB), BF16),
        V((16, JD), BF16), V((16, 128), F32), V((16, 128), F32), dma((7,)),
        V((16, JD), F32), V((3, 16, JD), F32), dma, dma((3,)),
        V((4, 16, 128), F32), V((3, 16, 128), F32), dma, dma((3,)),
        V((CH, 4, 8, JD), F32), V((CH, 3, 8, JD), F32), dma, dma((CH,)),
        V((LB, JD), F32), V((2048, 128), F32), V((2048, 128), F32), V((2048, 128), F32), V((LB, VOCAB), F32),
        V((FR, 8, JD), F32),
        V((2048, JD), BF16), V((2, CELLS, VOCAB), F32), V((2048, VOCAB), BF16), V((CELLS, JD), F32),
        V((8, 4, JD), F32), V((7, 4, JD), F32), dma, dma,
        V((LB, JD), F32), V((3, 16, JD), F32), dma, dma,
        V((16, JD), F32), V((3, 16, JD), F32), dma, dma,
        V((16, JD), F32), V((16, JD), F32), dma, dma,
        V((2, 4, 2, 32, 8, 128), F32), V((4, 32, 8, 128), F32),
        V((4, 2, 32, 8, 128), F32), V((4, 32, 8, 128), F32), dma, dma((4,)), dma, dma((4,)),
        V((4, 3, 8, 8, 128), F32), V((3, 32, 8, 128), F32), V((4, 7, 4, 8, 128), F32),
        dma((3,)), dma((4,)), dma, dma((4,)),
        V((4, 8, 8, 128), F32), V((32, 8, 128), F32), V((4, 4, 8, 128), F32),
        V((3, 8, 8, 128), F32), V((3, 8, 8, 128), F32), V((3, 4, 8, 128), F32), dma((3,)), dma((3,)),
        V((2, 8, 2, 4, 128), F32), V((4, 2, 4, 128), F32), V((2, 7, 4, 128), F32), V((2, 8, 4, 128), F32),
        V((3, 4, 128), F32), V((4, 4, 128), F32), dma((4,)), dma((4,)), dma((2,)),
        V((2, 3, 4, 128), F32),
    ]
    hbm = pl.BlockSpec(memory_space=pl.ANY)
    vmem = pl.BlockSpec(memory_space=pltpu.VMEM)
    smem = pl.BlockSpec(memory_space=pltpu.SMEM)
    shapes = (
        jax.ShapeDtypeStruct((4, JD), F32),
        jax.ShapeDtypeStruct((16, JD), F32),
        jax.ShapeDtypeStruct((4, JD), F32),
    )
    results = pl.pallas_call(
        kernel,
        out_shape=shapes,
        in_specs=[hbm] * 7 + [smem],
        out_specs=(vmem, vmem, vmem),
        scratch_shapes=scratch,
        compiler_params=pltpu.CompilerParams(
            collective_id=0, has_side_effects=True, vmem_limit_bytes=60 * 1024 * 1024
        ),
    )(features, up_weight, down_weight, predictor, out_weight, blank_weight.T, label_weight.T, targets)
    return pl.pallas_call(
        hand_on, out_shape=shapes, in_specs=[vmem] * 3, out_specs=(vmem,) * 3
    )(*results)


def solution(mesh):
    placed = (
        P("frames", None),
        P(None, "hidden"),
        P("hidden", None),
        P(("labels", "hidden"), None),
        P(),
        P("frames", ("labels", "hidden")),
        P("frames", ("labels", "hidden")),
        P(("labels", "hidden")),
    )
    return jax.shard_map(
        on_device,
        mesh=mesh,
        in_specs=placed,
        out_specs=(
            P(("frames", "labels", "hidden"), None),
            P(("labels", "hidden"), None),
            P(("frames", "labels", "hidden"), None),
        ),
        check_vma=False,
    )
```
